256 devices in a mesh: dp: 32 (over z, x), mp: 8 (over y, core).
Axes of the slice: x: 4, y: 4, z: 8, core: 2. Of those that a mesh axis runs over, the one named last changes fastest.
Arguments:
- tokens: bfloat16 [32768, 8192], P('dp', 'mp'), may hold values from -6 to 6
- value_weight: bfloat16 [8192, 1024], P('mp'), may hold values from -0.0625 to 0.0625
- adapter_down_panels: bfloat16 [96, 64, 8192], P('dp', None, 'mp'), may hold values from -0.0625 to 0.0625
- adapter_up_panels: bfloat16 [96, 64, 1024], P('dp', None, 'mp'), may hold values from -0.75 to 0.75
- cotangent: bfloat16 [32768, 1024], P('dp', 'mp'), may hold values from -6 to 6
- block_list_entry: int32 [1024], P('dp'), may hold values from 0 to 31, as said below
- device_tenant_list: int32 [1024], P('dp'), may hold values from 0 to 95, as said below
- tenant_location_map: int32 [96], replicated, may hold values from 0 to 95, as said below
Outputs:
- values: bfloat16 [32768, 1024], P('dp', 'mp')
- token_gradient: bfloat16 [32768, 8192], P('dp', 'mp')
- grad_a: bfloat16 [96, 64, 8192], P('dp', None, 'mp')
- grad_b: bfloat16 [96, 64, 1024], P('dp', None, 'mp')
The draws below stay inside these ranges and needn't reach their ends.
Inputs may be any that keep to these rules, and one draw needn't show every extreme that they name: `device_tenant_list`: each entry names a tenant; no tenant stands twice in one list. Of one device's 32 entries, at most 2 name tenants whose storage location tenant_location_map[t] lies on one dp index (tenant_location_map[t] // 3), and every device's list has 2 entries on some one dp index. A permutation: tenant t's panels are row tenant_location_map[t] of adapter_down_panels and adapter_up_panels. `block_list_entry`: every entry of a device's tenant list is named by at least one of that device's row blocks.
All inputs are finite; a program needn't handle non-finite values.
Results may differ from the reference program's by a relative error of at most 0.0057.
Values may be sent and summed in bfloat16 or wider, within the bound.
A program may use at most 128 MiB of HBM per device.

```python
import jax
import jax.numpy as jnp
from jax import lax

MODEL_WIDTH = 8192
VALUE_WIDTH = 1024
ADAPTER_RANK = 64
BLK = 32
MOST = 2
ADP_DEV = 3
BLOCKS_DEV = 32
ROWS = 32768
TENANT_TOTAL = 96
LIST = 32
N_DP = 32


def lists_and_owners(key):
    owner_count = TENANT_TOTAL // ADP_DEV
    spots = owner_count * MOST
    placement = jax.random.permutation(jax.random.fold_in(key, 7), TENANT_TOTAL).astype(jnp.int32)
    tenant_at = jnp.argsort(placement).astype(jnp.int32)

    def one_list(device_key):
        key_one, key_two, key_three = jax.random.split(device_key, 3)
        order = jax.random.permutation(key_one, spots).astype(jnp.int32)
        holders = order // MOST
        first = holders[0]
        score = jnp.where(holders == first, 1, 0) * spots + jnp.arange(spots, dtype=jnp.int32)
        others = holders[jnp.argsort(score)][:LIST - 2]
        chosen = jnp.concatenate([jnp.stack([first, first]), others])
        chosen = chosen[jax.random.permutation(key_two, LIST)]
        entry_ids = jnp.arange(LIST, dtype=jnp.int32)
        same_holder = (chosen[:, None] == chosen[None, :]) & (entry_ids[:, None] > entry_ids[None, :])
        earlier_count = jnp.sum(jnp.where(same_holder, 1, 0), axis=1).astype(jnp.int32)
        start_row = jax.random.randint(key_three, (owner_count,), 0, ADP_DEV).astype(jnp.int32)
        local_row = (start_row[chosen] + earlier_count) % ADP_DEV
        return tenant_at[chosen * ADP_DEV + local_row]
    device_keys = jax.random.split(jax.random.fold_in(key, 8), owner_count)
    lists = jax.vmap(one_list)(device_keys).reshape(-1).astype(jnp.int32)
    return (lists, placement)


def draw_device_tenant_list(key, part):
    return lists_and_owners(key)[0]


def draw_tenant_location_map(key, part):
    return lists_and_owners(key)[1]


def draw_block_list_entry(key, part):
    owner_count = TENANT_TOTAL // ADP_DEV
    extra_count = BLOCKS_DEV - LIST

    def one_device(device_key):
        key_one, key_two, key_three, key_four = jax.random.split(device_key, 4)
        cover = jax.random.permutation(key_one, LIST).astype(jnp.int32)
        first_pick = jax.random.randint(key_two, (extra_count,), 0, LIST).astype(jnp.int32)
        second_pick = jax.random.randint(key_three, (extra_count,), 0, LIST).astype(jnp.int32)
        extra = jnp.minimum(first_pick, second_pick)
        joined = jnp.concatenate([cover, extra])
        return joined[jax.random.permutation(key_four, BLOCKS_DEV)]
    device_keys = jax.random.split(jax.random.fold_in(key, 9), owner_count)
    return jax.vmap(one_device)(device_keys).reshape(-1).astype(jnp.int32)


def block_levels(own_key, shape, shards, low, top_value):
    gain, own = 1.0, jax.random.fold_in(own_key, 6)
    for axis_at, blocks in shards:
        draws = jnp.exp(jax.random.uniform(jax.random.fold_in(own, axis_at), (blocks,), jnp.float32, low / len(shards), top_value / len(shards)))
        gain = gain * jnp.repeat(draws, shape[axis_at] // blocks).reshape([-1 if axis == axis_at else 1 for axis in range(len(shape))])
    return gain


def noise(own_key, dims, deviation, reach, cuts=(), kind=jnp.bfloat16):
    drawn = jax.random.normal(own_key, dims, jnp.float32) * deviation
    if len(cuts) > 0:
        drawn = block_levels(own_key, dims, cuts, -0.22, 0.18) * drawn
    return jnp.clip(drawn, min=-reach, max=reach).astype(kind)


def setup_inputs(seed: int = 0) -> dict:
    seeds = jax.random.split(jax.random.key(seed), 9)
    return {
        "tokens": noise(seeds[0], (ROWS, MODEL_WIDTH), 1.0, 6.0, ((0, 32), (1, 8))),
        "value_weight": noise(seeds[1], (MODEL_WIDTH, VALUE_WIDTH), MODEL_WIDTH ** -0.5, 0.0625, ((0, 8),)),
        "adapter_down_panels": noise(seeds[2], (TENANT_TOTAL, ADAPTER_RANK, MODEL_WIDTH), MODEL_WIDTH ** -0.5, 0.0625, ((0, 32), (2, 8))),
        "adapter_up_panels": noise(seeds[3], (TENANT_TOTAL, ADAPTER_RANK, VALUE_WIDTH), ADAPTER_RANK ** -0.5, 0.75, ((0, 32), (2, 8))),
        "cotangent": noise(seeds[4], (ROWS, VALUE_WIDTH), 1.0, 6.0, ((0, 32), (1, 8))),
        "block_list_entry": draw_block_list_entry(jax.random.fold_in(seeds[8], 71), 0),
        "device_tenant_list": draw_device_tenant_list(jax.random.fold_in(seeds[8], 71), 0),
        "tenant_location_map": draw_tenant_location_map(jax.random.fold_in(seeds[8], 71), 0),
    }


def reference(tokens, value_weight, adapter_down_panels, adapter_up_panels, cotangent, block_list_entry, device_tenant_list, tenant_location_map):
    token_dev = tokens.reshape(N_DP, BLOCKS_DEV, BLK, MODEL_WIDTH)
    cot_dev = cotangent.reshape(N_DP, BLOCKS_DEV, BLK, VALUE_WIDTH)
    slot_dev = block_list_entry.reshape(N_DP, BLOCKS_DEV)
    list_dev = device_tenant_list.reshape(N_DP, LIST)
    stored_ids = jnp.arange(TENANT_TOTAL, dtype=jnp.int32)

    def one_device(carry, items):
        total_a, total_b = carry
        token_blocks, cot_blocks, slot_row, list_row = items
        tenant = jnp.take(list_row, slot_row.astype(jnp.int32)).astype(jnp.int32)
        storage_location = jnp.take(tenant_location_map, tenant).astype(jnp.int32)
        block_down_panel = jnp.take(adapter_down_panels, storage_location, axis=0).astype(jnp.float32)
        block_up_panel = jnp.take(adapter_up_panels, storage_location, axis=0).astype(jnp.float32)
        token_f = token_blocks.astype(jnp.float32)
        cot_f = cot_blocks.astype(jnp.float32)
        base_output = jnp.dot(token_blocks.reshape(-1, MODEL_WIDTH), value_weight, preferred_element_type=jnp.float32)
        down_low = jnp.einsum("bnd,brd->bnr", token_f, block_down_panel).astype(jnp.bfloat16)
        down_forward = lax.optimization_barrier(down_low).astype(jnp.float32)
        adapter_output = jnp.einsum("afq,aqy->afy", down_forward, block_up_panel).reshape(-1, VALUE_WIDTH)
        values = (base_output + adapter_output).astype(jnp.bfloat16)
        up_grad = jnp.einsum("bnc,brc->bnr", cot_f, block_up_panel).astype(jnp.bfloat16)
        up_forward = lax.optimization_barrier(up_grad).astype(jnp.float32)
        base_backward_pass = jnp.dot(cot_blocks.reshape(-1, VALUE_WIDTH), value_weight.T, preferred_element_type=jnp.float32)
        adapter_backward_pass = jnp.einsum("swq,sqj->swj", up_forward, block_down_panel).reshape(-1, MODEL_WIDTH)
        token_gradient = (base_backward_pass + adapter_backward_pass).astype(jnp.bfloat16)
        block_grad_a = jnp.einsum("bnr,bnd->brd", up_forward, token_f)
        block_grad_b = jnp.einsum("bnr,bnc->brc", down_forward, cot_f)
        picker = (stored_ids[:, None] == storage_location[None, :]).astype(jnp.float32)
        share_a = jnp.einsum("lb,brd->lrd", picker, block_grad_a, precision=lax.Precision.HIGHEST).astype(jnp.bfloat16)
        share_b = jnp.einsum("lb,brc->lrc", picker, block_grad_b, precision=lax.Precision.HIGHEST).astype(jnp.bfloat16)
        share_a = lax.optimization_barrier(share_a).astype(jnp.float32)
        share_b = lax.optimization_barrier(share_b).astype(jnp.float32)
        return (total_a + share_a, total_b + share_b), (values, token_gradient)

    start = (jnp.zeros((TENANT_TOTAL, ADAPTER_RANK, MODEL_WIDTH), jnp.float32), jnp.zeros((TENANT_TOTAL, ADAPTER_RANK, VALUE_WIDTH), jnp.float32))
    totals, outputs = lax.scan(one_device, start, (token_dev, cot_dev, slot_dev, list_dev))
    values = outputs[0].reshape(ROWS, VALUE_WIDTH)
    token_gradient = outputs[1].reshape(ROWS, MODEL_WIDTH)
    return values, token_gradient, totals[0].astype(jnp.bfloat16), totals[1].astype(jnp.bfloat16)
```

```python
import jax
import jax.numpy as jnp
from jax import lax
from jax.sharding import PartitionSpec as P

MOST = 2


def earlier_same(holder):
    count = holder.shape[-1]
    ids = jnp.arange(count, dtype=jnp.int32)
    same = (holder[..., :, None] == holder[..., None, :]) & (ids[:, None] > ids[None, :])
    return jnp.sum(same.astype(jnp.int32), axis=-1)


def shards(
    tokens,
    value_weight,
    adapter_down_panels,
    adapter_up_panels,
    cotangent,
    block_list_entry,
    device_tenant_list,
    tenant_location_map,
):
    rows, width_loc = tokens.shape
    stored, rank, _ = adapter_down_panels.shape
    out_loc = adapter_up_panels.shape[2]
    blocks = block_list_entry.shape[0]
    blk = rows // blocks
    n_dp = lax.axis_size("dp")
    capacity = n_dp * MOST
    me = lax.axis_index("dp")

    tenant = jnp.take(device_tenant_list, block_list_entry, mode="clip")
    location = jnp.take(tenant_location_map, tenant, mode="clip")
    holder = location // stored
    position = holder * MOST + earlier_same(holder)

    slot_ids = jnp.arange(capacity, dtype=jnp.int32)
    block_ids = jnp.arange(blocks, dtype=jnp.int32)
    source = jnp.sum(
        jnp.where(position[None, :] == slot_ids[:, None], block_ids[None, :], 0), axis=1
    )

    all_location = lax.all_gather(location, "dp", axis=0, tiled=False)
    all_holder = all_location // stored
    all_rank = earlier_same(all_holder)
    mine = all_holder == me
    slot_row = jnp.stack(
        [
            jnp.sum(jnp.where(mine & (all_rank == r), all_location % stored + 1, 0), axis=1)
            for r in range(MOST)
        ],
        axis=1,
    ).reshape(capacity) - 1
    pick = slot_row[:, None] == jnp.arange(stored, dtype=jnp.int32)[None, :]

    base_t = lax.psum_scatter(
        lax.dot_general(
            value_weight, tokens, (((0,), (1,)), ((), ())), preferred_element_type=jnp.float32
        ),
        "mp",
        scatter_dimension=0,
        tiled=True,
    )
    cot_full = lax.all_gather(cotangent, "mp", axis=1, tiled=True)
    base_bwd = lax.dot_general(
        cot_full, value_weight, (((1,), (1,)), ((), ())), preferred_element_type=jnp.float32
    )

    token_blocks = tokens.reshape(blocks, blk, width_loc)
    cot_blocks = cotangent.reshape(blocks, blk, out_loc)
    send = jnp.concatenate(
        [jnp.take(token_blocks, source, axis=0), jnp.take(cot_blocks, source, axis=0)], axis=2
    )
    recv = lax.all_to_all(send, "dp", split_axis=0, concat_axis=0, tiled=True)
    recv_rows = recv.reshape(capacity * blk, width_loc + out_loc)
    tok_recv = recv_rows[:, :width_loc]
    cot_recv = recv_rows[:, width_loc:]

    down_flat = adapter_down_panels.reshape(stored * rank, width_loc)
    up_flat = adapter_up_panels.reshape(stored * rank, out_loc)
    pick_rows = jnp.broadcast_to(pick[:, None, :, None], (capacity, blk, stored, rank)).reshape(
        capacity * blk, stored * rank
    )

    def select(all_cols):
        parts = jnp.where(pick_rows, all_cols, 0.0).reshape(capacity * blk, stored, rank)
        return jnp.sum(parts, axis=1)

    down_part = select(
        lax.dot_general(tok_recv, down_flat, (((1,), (1,)), ((), ())), preferred_element_type=jnp.float32)
    )
    up_part = select(
        lax.dot_general(cot_recv, up_flat, (((1,), (1,)), ((), ())), preferred_element_type=jnp.float32)
    )
    both = lax.psum(jnp.stack([down_part, up_part]), "mp").astype(jnp.bfloat16)
    down_low = both[0]
    up_grad = both[1]

    def spread(small):
        wide = jnp.broadcast_to(small[:, None, :], (capacity * blk, stored, rank)).reshape(
            capacity * blk, stored * rank
        )
        return jnp.where(pick_rows, wide, jnp.zeros_like(wide))

    down_wide = spread(down_low)
    up_wide = spread(up_grad)

    adapter_out = jnp.dot(down_wide, up_flat, preferred_element_type=jnp.float32)
    adapter_bwd = jnp.dot(up_wide, down_flat, preferred_element_type=jnp.float32)
    back_send = jnp.concatenate(
        [adapter_bwd.astype(jnp.bfloat16), adapter_out.astype(jnp.bfloat16)], axis=1
    ).reshape(capacity, blk, width_loc + out_loc)

    grad_a = lax.dot_general(
        up_wide, tok_recv, (((0,), (0,)), ((), ())), preferred_element_type=jnp.float32
    ).astype(jnp.bfloat16).reshape(stored, rank, width_loc)
    grad_b = lax.dot_general(
        down_wide, cot_recv, (((0,), (0,)), ((), ())), preferred_element_type=jnp.float32
    ).astype(jnp.bfloat16).reshape(stored, rank, out_loc)

    back = lax.all_to_all(back_send, "dp", split_axis=0, concat_axis=0, tiled=True)
    mine_back = jnp.take(back, position, axis=0).reshape(rows, width_loc + out_loc)

    values = (base_t.T + mine_back[:, width_loc:].astype(jnp.float32)).astype(jnp.bfloat16)
    token_gradient = (base_bwd + mine_back[:, :width_loc].astype(jnp.float32)).astype(jnp.bfloat16)
    return (values, token_gradient, grad_a, grad_b)


def solution(mesh):
    in_specs = (
        P("dp", "mp"),
        P("mp", None),
        P("dp", None, "mp"),
        P("dp", None, "mp"),
        P("dp", "mp"),
        P("dp"),
        P("dp"),
        P(),
    )
    out_specs = (P("dp", "mp"), P("dp", "mp"), P("dp", None, "mp"), P("dp", None, "mp"))
    return jax.shard_map(shards, mesh=mesh, in_specs=in_specs, out_specs=out_specs, check_vma=False)
```

```python
import jax
import jax.numpy as jnp
from jax import lax
from jax.sharding import PartitionSpec as P

MOST = 2


def earlier_same(holder):
    count = holder.shape[-1]
    ids = jnp.arange(count, dtype=jnp.int32)
    same = (holder[..., :, None] == holder[..., None, :]) & (ids[:, None] > ids[None, :])
    return jnp.sum(same.astype(jnp.int32), axis=-1)


def shards(
    tokens,
    value_weight,
    adapter_down_panels,
    adapter_up_panels,
    cotangent,
    block_list_entry,
    device_tenant_list,
    tenant_location_map,
):
    rows, width_loc = tokens.shape
    stored, rank, _ = adapter_down_panels.shape
    out_loc = adapter_up_panels.shape[2]
    blocks = block_list_entry.shape[0]
    blk = rows // blocks
    n_dp = lax.axis_size("dp")
    capacity = n_dp * MOST
    me = lax.axis_index("dp")

    tenant = jnp.take(device_tenant_list, block_list_entry, mode="clip")
    location = jnp.take(tenant_location_map, tenant, mode="clip")
    holder = location // stored
    position = holder * MOST + earlier_same(holder)

    slot_ids = jnp.arange(capacity, dtype=jnp.int32)
    block_ids = jnp.arange(blocks, dtype=jnp.int32)
    source = jnp.sum(
        jnp.where(position[None, :] == slot_ids[:, None], block_ids[None, :], 0), axis=1
    )

    all_location = lax.all_gather(location, "dp", axis=0, tiled=False)
    all_holder = all_location // stored
    all_rank = earlier_same(all_holder)
    mine = all_holder == me
    slot_row = jnp.stack(
        [
            jnp.sum(jnp.where(mine & (all_rank == r), all_location % stored + 1, 0), axis=1)
            for r in range(MOST)
        ],
        axis=1,
    ).reshape(capacity) - 1
    pick = slot_row[:, None] == jnp.arange(stored, dtype=jnp.int32)[None, :]

    base_t = lax.psum_scatter(
        lax.dot_general(
            value_weight, tokens, (((0,), (1,)), ((), ())), preferred_element_type=jnp.float32
        ),
        "mp",
        scatter_dimension=0,
        tiled=True,
    )
    cot_full = lax.all_gather(cotangent, "mp", axis=1, tiled=True)
    base_bwd = lax.dot_general(
        cot_full, value_weight, (((1,), (1,)), ((), ())), preferred_element_type=jnp.float32
    )

    token_blocks = tokens.reshape(blocks, blk, width_loc)
    cot_blocks = cotangent.reshape(blocks, blk, out_loc)
    send = jnp.concatenate(
        [jnp.take(token_blocks, source, axis=0), jnp.take(cot_blocks, source, axis=0)], axis=2
    )
    recv = lax.all_to_all(send, "dp", split_axis=0, concat_axis=0, tiled=True)
    recv_rows = recv.reshape(capacity * blk, width_loc + out_loc)
    tok_recv = recv_rows[:, :width_loc]
    cot_recv = recv_rows[:, width_loc:]

    down_flat = adapter_down_panels.reshape(stored * rank, width_loc)
    up_flat = adapter_up_panels.reshape(stored * rank, out_loc)
    pick_rows = jnp.broadcast_to(pick[:, None, :, None], (capacity, blk, stored, rank)).reshape(
        capacity * blk, stored * rank
    )

    def select(all_cols):
        parts = jnp.where(pick_rows, all_cols, 0.0).reshape(capacity * blk, stored, rank)
        return jnp.sum(parts, axis=1)

    down_part = select(
        lax.dot_general(tok_recv, down_flat, (((1,), (1,)), ((), ())), preferred_element_type=jnp.float32)
    )
    up_part = select(
        lax.dot_general(cot_recv, up_flat, (((1,), (1,)), ((), ())), preferred_element_type=jnp.float32)
    )
    both = lax.all_gather(
        lax.psum_scatter(jnp.stack([down_part, up_part]), "mp", scatter_dimension=1, tiled=True).astype(
            jnp.bfloat16
        ),
        "mp",
        axis=1,
        tiled=True,
    )
    down_low = both[0]
    up_grad = both[1]

    def spread(small):
        wide = jnp.broadcast_to(small[:, None, :], (capacity * blk, stored, rank)).reshape(
            capacity * blk, stored * rank
        )
        return jnp.where(pick_rows, wide, jnp.zeros_like(wide))

    down_wide = spread(down_low)
    up_wide = spread(up_grad)

    adapter_out = jnp.dot(down_wide, up_flat, preferred_element_type=jnp.float32)
    adapter_bwd = jnp.dot(up_wide, down_flat, preferred_element_type=jnp.float32)
    back_send = jnp.concatenate(
        [adapter_bwd.astype(jnp.bfloat16), adapter_out.astype(jnp.bfloat16)], axis=1
    ).reshape(capacity, blk, width_loc + out_loc)

    grad_a = lax.dot_general(
        up_wide, tok_recv, (((0,), (0,)), ((), ())), preferred_element_type=jnp.float32
    ).astype(jnp.bfloat16).reshape(stored, rank, width_loc)
    grad_b = lax.dot_general(
        down_wide, cot_recv, (((0,), (0,)), ((), ())), preferred_element_type=jnp.float32
    ).astype(jnp.bfloat16).reshape(stored, rank, out_loc)

    back = lax.all_to_all(back_send, "dp", split_axis=0, concat_axis=0, tiled=True)
    mine_back = jnp.take(back, position, axis=0).reshape(rows, width_loc + out_loc)

    values = (base_t.T + mine_back[:, width_loc:].astype(jnp.float32)).astype(jnp.bfloat16)
    token_gradient = (base_bwd + mine_back[:, :width_loc].astype(jnp.float32)).astype(jnp.bfloat16)
    return (values, token_gradient, grad_a, grad_b)


def solution(mesh):
    in_specs = (
        P("dp", "mp"),
        P("mp", None),
        P("dp", None, "mp"),
        P("dp", None, "mp"),
        P("dp", "mp"),
        P("dp"),
        P("dp"),
        P(),
    )
    out_specs = (P("dp", "mp"), P("dp", "mp"), P("dp", None, "mp"), P("dp", None, "mp"))
    return jax.shard_map(shards, mesh=mesh, in_specs=in_specs, out_specs=out_specs, check_vma=False)
```

```python
import jax
import jax.numpy as jnp
from jax import lax
from jax.sharding import PartitionSpec as P

MOST = 2


def earlier_same(holder):
    count = holder.shape[-1]
    ids = jnp.arange(count, dtype=jnp.int32)
    same = (holder[..., :, None] == holder[..., None, :]) & (ids[:, None] > ids[None, :])
    return jnp.sum(same.astype(jnp.int32), axis=-1)


def shards(
    tokens,
    value_weight,
    adapter_down_panels,
    adapter_up_panels,
    cotangent,
    block_list_entry,
    device_tenant_list,
    tenant_location_map,
):
    rows, width_loc = tokens.shape
    stored, rank, _ = adapter_down_panels.shape
    out_loc = adapter_up_panels.shape[2]
    blocks = block_list_entry.shape[0]
    blk = rows // blocks
    n_dp = lax.axis_size("dp")
    capacity = n_dp * MOST
    me = lax.axis_index("dp")

    tenant = jnp.take(device_tenant_list, block_list_entry, mode="clip")
    location = jnp.take(tenant_location_map, tenant, mode="clip")
    holder = location // stored
    position = holder * MOST + earlier_same(holder)

    slot_ids = jnp.arange(capacity, dtype=jnp.int32)
    block_ids = jnp.arange(blocks, dtype=jnp.int32)
    source = jnp.sum(
        jnp.where(position[None, :] == slot_ids[:, None], block_ids[None, :], 0), axis=1
    )

    all_location = lax.all_gather(location, "dp", axis=0, tiled=False)
    all_holder = all_location // stored
    all_rank = earlier_same(all_holder)
    mine = all_holder == me
    slot_row = jnp.stack(
        [
            jnp.sum(jnp.where(mine & (all_rank == r), all_location % stored + 1, 0), axis=1)
            for r in range(MOST)
        ],
        axis=1,
    ).reshape(capacity) - 1

    base_t = lax.psum_scatter(
        lax.dot_general(
            value_weight, tokens, (((0,), (1,)), ((), ())), preferred_element_type=jnp.float32
        ),
        "mp",
        scatter_dimension=0,
        tiled=True,
    )
    cot_full = lax.all_gather(cotangent, "mp", axis=1, tiled=True)
    base_bwd = lax.dot_general(
        cot_full, value_weight, (((1,), (1,)), ((), ())), preferred_element_type=jnp.float32
    )

    token_blocks = tokens.reshape(blocks, blk, width_loc)
    cot_blocks = cotangent.reshape(blocks, blk, out_loc)
    send = jnp.concatenate(
        [jnp.take(token_blocks, source, axis=0), jnp.take(cot_blocks, source, axis=0)], axis=2
    )
    down_flat = adapter_down_panels.reshape(stored * rank, width_loc)
    up_flat = adapter_up_panels.reshape(stored * rank, out_loc)
    send = send.reshape(n_dp, MOST, blk, width_loc + out_loc)
    slot_row = slot_row.reshape(n_dp, MOST)
    backs = []
    grad_a = 0.0
    grad_b = 0.0
    for r in range(MOST):
        recv = lax.all_to_all(send[:, r], "dp", split_axis=0, concat_axis=0, tiled=True)
        recv_rows = recv.reshape(n_dp * blk, width_loc + out_loc)
        tok_recv = recv_rows[:, :width_loc]
        cot_recv = recv_rows[:, width_loc:]
        pick = slot_row[:, r][:, None] == jnp.arange(stored, dtype=jnp.int32)[None, :]
        pick_rows = jnp.broadcast_to(pick[:, None, :, None], (n_dp, blk, stored, rank)).reshape(
            n_dp * blk, stored * rank
        )

        def select(all_cols):
            parts = jnp.where(pick_rows, all_cols, 0.0).reshape(n_dp * blk, stored, rank)
            return jnp.sum(parts, axis=1)

        down_part = select(
            lax.dot_general(tok_recv, down_flat, (((1,), (1,)), ((), ())), preferred_element_type=jnp.float32)
        )
        up_part = select(
            lax.dot_general(cot_recv, up_flat, (((1,), (1,)), ((), ())), preferred_element_type=jnp.float32)
        )
        both = lax.all_gather(
            lax.psum_scatter(jnp.stack([down_part, up_part]), "mp", scatter_dimension=1, tiled=True).astype(
                jnp.bfloat16
            ),
            "mp",
            axis=1,
            tiled=True,
        )

        def spread(small):
            wide = jnp.broadcast_to(small[:, None, :], (n_dp * blk, stored, rank)).reshape(
                n_dp * blk, stored * rank
            )
            return jnp.where(pick_rows, wide, jnp.zeros_like(wide))

        down_wide = spread(both[0])
        up_wide = spread(both[1])
        adapter_out = jnp.dot(down_wide, up_flat, preferred_element_type=jnp.float32)
        adapter_bwd = jnp.dot(up_wide, down_flat, preferred_element_type=jnp.float32)
        back_send = jnp.concatenate(
            [adapter_bwd.astype(jnp.bfloat16), adapter_out.astype(jnp.bfloat16)], axis=1
        ).reshape(n_dp, blk, width_loc + out_loc)
        backs.append(lax.all_to_all(back_send, "dp", split_axis=0, concat_axis=0, tiled=True))
        grad_a = grad_a + lax.dot_general(
            up_wide, tok_recv, (((0,), (0,)), ((), ())), preferred_element_type=jnp.float32
        )
        grad_b = grad_b + lax.dot_general(
            down_wide, cot_recv, (((0,), (0,)), ((), ())), preferred_element_type=jnp.float32
        )
    grad_a = grad_a.astype(jnp.bfloat16).reshape(stored, rank, width_loc)
    grad_b = grad_b.astype(jnp.bfloat16).reshape(stored, rank, out_loc)
    back = jnp.stack(backs, axis=1).reshape(capacity, blk, width_loc + out_loc)
    mine_back = jnp.take(back, position, axis=0).reshape(rows, width_loc + out_loc)

    values = (base_t.T + mine_back[:, width_loc:].astype(jnp.float32)).astype(jnp.bfloat16)
    token_gradient = (base_bwd + mine_back[:, :width_loc].astype(jnp.float32)).astype(jnp.bfloat16)
    return (values, token_gradient, grad_a, grad_b)


def solution(mesh):
    in_specs = (
        P("dp", "mp"),
        P("mp", None),
        P("dp", None, "mp"),
        P("dp", None, "mp"),
        P("dp", "mp"),
        P("dp"),
        P("dp"),
        P(),
    )
    out_specs = (P("dp", "mp"), P("dp", "mp"), P("dp", None, "mp"), P("dp", None, "mp"))
    return jax.shard_map(shards, mesh=mesh, in_specs=in_specs, out_specs=out_specs, check_vma=False)
```

```python
import jax
import jax.numpy as jnp
import numpy as np
from jax import lax
from jax.sharding import Mesh
from jax.sharding import PartitionSpec as P

MOST = 2
DP = ("dz", "dx")


def earlier_same(group):
    count = group.shape[-1]
    ids = jnp.arange(count, dtype=jnp.int32)
    same = (group[..., :, None] == group[..., None, :]) & (ids[:, None] > ids[None, :])
    return jnp.sum(same.astype(jnp.int32), axis=-1)


def shards(
    tokens,
    value_weight,
    adapter_down_panels,
    adapter_up_panels,
    cotangent,
    block_list_entry,
    device_tenant_list,
    tenant_location_map,
):
    rows, width_loc = tokens.shape
    stored, rank, _ = adapter_down_panels.shape
    out_loc = adapter_up_panels.shape[2]
    blocks = block_list_entry.shape[0]
    blk = rows // blocks
    n_z = lax.axis_size("dz")
    n_x = lax.axis_size("dx")
    per_x = min(MOST * n_z, blocks)
    capacity = n_x * per_x
    my_x = lax.axis_index("dx")
    column = n_z * stored

    tenant = jnp.take(device_tenant_list, block_list_entry, mode="clip")
    location = jnp.take(tenant_location_map, tenant, mode="clip")
    owner_x = (location // stored) % n_x
    position = owner_x * per_x + earlier_same(owner_x)

    slot_ids = jnp.arange(capacity, dtype=jnp.int32)
    block_ids = jnp.arange(blocks, dtype=jnp.int32)
    source = jnp.sum(
        jnp.where(position[None, :] == slot_ids[:, None], block_ids[None, :], 0), axis=1
    )

    x_location = lax.all_gather(location, "dx", axis=0, tiled=False)
    x_owner_x = (x_location // stored) % n_x
    x_rank = earlier_same(x_owner_x)
    in_column = (x_location // stored // n_x) * stored + x_location % stored
    mine = x_owner_x == my_x
    slot_panel = jnp.stack(
        [jnp.sum(jnp.where(mine & (x_rank == c), in_column + 1, 0), axis=1) for c in range(per_x)],
        axis=1,
    ).reshape(capacity) - 1
    pick = slot_panel[:, None] == jnp.arange(column, dtype=jnp.int32)[None, :]

    down_col = lax.all_gather(adapter_down_panels, "dz", axis=0, tiled=True)
    up_col = lax.all_gather(adapter_up_panels, "dz", axis=0, tiled=True)

    base_t = lax.psum_scatter(
        lax.dot_general(
            value_weight, tokens, (((0,), (1,)), ((), ())), preferred_element_type=jnp.float32
        ),
        "mp",
        scatter_dimension=0,
        tiled=True,
    )
    cot_full = lax.all_gather(cotangent, "mp", axis=1, tiled=True)
    base_bwd = lax.dot_general(
        cot_full, value_weight, (((1,), (1,)), ((), ())), preferred_element_type=jnp.float32
    )

    token_blocks = tokens.reshape(blocks, blk, width_loc)
    cot_blocks = cotangent.reshape(blocks, blk, out_loc)
    send = jnp.concatenate(
        [jnp.take(token_blocks, source, axis=0), jnp.take(cot_blocks, source, axis=0)], axis=2
    )
    recv = lax.all_to_all(send, "dx", split_axis=0, concat_axis=0, tiled=True)
    tok_recv = recv[:, :, :width_loc]
    cot_recv = recv[:, :, width_loc:]

    panel_at = jnp.clip(slot_panel, 0, column - 1)
    down_sel = jnp.take(down_col, panel_at, axis=0)
    up_sel = jnp.take(up_col, panel_at, axis=0)
    down_part = jnp.einsum("snd,srd->snr", tok_recv, down_sel, preferred_element_type=jnp.float32)
    up_part = jnp.einsum("snc,src->snr", cot_recv, up_sel, preferred_element_type=jnp.float32)
    both = lax.all_gather(
        lax.psum_scatter(jnp.stack([down_part, up_part]), "mp", scatter_dimension=1, tiled=True).astype(
            jnp.bfloat16
        ),
        "mp",
        axis=1,
        tiled=True,
    )
    down_low = both[0]
    up_grad = both[1]

    adapter_out = jnp.einsum("snr,src->snc", down_low, up_sel, preferred_element_type=jnp.float32)
    adapter_bwd = jnp.einsum("snr,srd->snd", up_grad, down_sel, preferred_element_type=jnp.float32)
    back_send = jnp.concatenate(
        [adapter_bwd.astype(jnp.bfloat16), adapter_out.astype(jnp.bfloat16)], axis=2
    )
    back = lax.all_to_all(back_send, "dx", split_axis=0, concat_axis=0, tiled=True)

    pick_rows = jnp.broadcast_to(pick[:, None, :, None], (capacity, blk, column, rank)).reshape(
        capacity * blk, column * rank
    )

    def spread(small):
        wide = jnp.broadcast_to(small.reshape(capacity * blk, 1, rank), (capacity * blk, column, rank))
        wide = wide.reshape(capacity * blk, column * rank)
        return jnp.where(pick_rows, wide, jnp.zeros_like(wide))

    grad_a_col = lax.dot_general(
        spread(up_grad),
        tok_recv.reshape(capacity * blk, width_loc),
        (((0,), (0,)), ((), ())),
        preferred_element_type=jnp.float32,
    )
    grad_b_col = lax.dot_general(
        spread(down_low),
        cot_recv.reshape(capacity * blk, out_loc),
        (((0,), (0,)), ((), ())),
        preferred_element_type=jnp.float32,
    )
    grad_a = lax.psum_scatter(grad_a_col, "dz", scatter_dimension=0, tiled=True)
    grad_b = lax.psum_scatter(grad_b_col, "dz", scatter_dimension=0, tiled=True)
    grad_a = grad_a.astype(jnp.bfloat16).reshape(stored, rank, width_loc)
    grad_b = grad_b.astype(jnp.bfloat16).reshape(stored, rank, out_loc)

    mine_back = jnp.take(back, position, axis=0).reshape(rows, width_loc + out_loc)
    values = (base_t.T + mine_back[:, width_loc:].astype(jnp.float32)).astype(jnp.bfloat16)
    token_gradient = (base_bwd + mine_back[:, :width_loc].astype(jnp.float32)).astype(jnp.bfloat16)
    return (values, token_gradient, grad_a, grad_b)


def split_dp(mesh):
    devices = np.asarray(mesh.devices)
    n_dp, n_mp = devices.shape
    try:
        n_x = len({tuple(d.coords)[0] for d in devices[:, 0]})
    except (AttributeError, TypeError):
        n_x = 1
    if n_x < 1 or n_dp % n_x:
        n_x = 1
    return Mesh(devices.reshape(n_dp // n_x, n_x, n_mp), ("dz", "dx", "mp"))


def solution(mesh):
    in_specs = (
        P(DP, "mp"),
        P("mp", None),
        P(DP, None, "mp"),
        P(DP, None, "mp"),
        P(DP, "mp"),
        P(DP),
        P(DP),
        P(),
    )
    out_specs = (P(DP, "mp"), P(DP, "mp"), P(DP, None, "mp"), P(DP, None, "mp"))
    return jax.shard_map(
        shards, mesh=split_dp(mesh), in_specs=in_specs, out_specs=out_specs, check_vma=False
    )
```

```python
import jax
import jax.numpy as jnp
import numpy as np
from jax import lax
from jax.sharding import Mesh
from jax.sharding import PartitionSpec as P

MOST = 2
DP = ("dz", "dx")


def earlier_same(group):
    count = group.shape[-1]
    ids = jnp.arange(count, dtype=jnp.int32)
    same = (group[..., :, None] == group[..., None, :]) & (ids[:, None] > ids[None, :])
    return jnp.sum(same.astype(jnp.int32), axis=-1)


def shards(
    tokens,
    value_weight,
    adapter_down_panels,
    adapter_up_panels,
    cotangent,
    block_list_entry,
    device_tenant_list,
    tenant_location_map,
):
    rows, width_loc = tokens.shape
    stored, rank, _ = adapter_down_panels.shape
    out_loc = adapter_up_panels.shape[2]
    blocks = block_list_entry.shape[0]
    blk = rows // blocks
    n_z = lax.axis_size("dz")
    n_x = lax.axis_size("dx")
    per_x = min(MOST * n_z, blocks)
    capacity = n_x * per_x
    my_x = lax.axis_index("dx")
    column = n_z * stored

    tenant = jnp.take(device_tenant_list, block_list_entry, mode="clip")
    location = jnp.take(tenant_location_map, tenant, mode="clip")
    owner_x = (location // stored) % n_x
    position = owner_x * per_x + earlier_same(owner_x)

    slot_ids = jnp.arange(capacity, dtype=jnp.int32)
    block_ids = jnp.arange(blocks, dtype=jnp.int32)
    source = jnp.sum(
        jnp.where(position[None, :] == slot_ids[:, None], block_ids[None, :], 0), axis=1
    )

    x_location = lax.all_gather(location, "dx", axis=0, tiled=False)
    x_owner_x = (x_location // stored) % n_x
    x_rank = earlier_same(x_owner_x)
    in_column = (x_location // stored // n_x) * stored + x_location % stored
    mine = x_owner_x == my_x
    slot_panel = jnp.stack(
        [jnp.sum(jnp.where(mine & (x_rank == c), in_column + 1, 0), axis=1) for c in range(per_x)],
        axis=1,
    ).reshape(capacity) - 1
    panel_ids = jnp.arange(column, dtype=jnp.int32)
    slot_of = x_rank + (jnp.arange(n_x, dtype=jnp.int32) * per_x)[:, None]
    panel_slot = jnp.sum(
        jnp.where(
            mine[None, :, :] & (in_column[None, :, :] == panel_ids[:, None, None]),
            slot_of[None, :, :] + 1,
            0,
        ),
        axis=2,
    ) - 1
    panel_used = panel_slot >= 0
    panel_slot = jnp.clip(panel_slot, 0, capacity - 1)

    both_col = lax.all_gather(
        jnp.concatenate([adapter_down_panels, adapter_up_panels], axis=2), "dz", axis=0, tiled=True
    )
    down_col = both_col[:, :, :width_loc]
    up_col = both_col[:, :, width_loc:]

    base_t = lax.psum_scatter(
        lax.dot_general(
            value_weight, tokens, (((0,), (1,)), ((), ())), preferred_element_type=jnp.float32
        ),
        "mp",
        scatter_dimension=0,
        tiled=True,
    )
    cot_full = lax.all_gather(cotangent, "mp", axis=1, tiled=True)
    base_bwd = lax.dot_general(
        cot_full, value_weight, (((1,), (1,)), ((), ())), preferred_element_type=jnp.float32
    )

    token_blocks = tokens.reshape(blocks, blk, width_loc)
    cot_blocks = cotangent.reshape(blocks, blk, out_loc)
    send = jnp.concatenate(
        [jnp.take(token_blocks, source, axis=0), jnp.take(cot_blocks, source, axis=0)], axis=2
    )
    recv = lax.all_to_all(send, "dx", split_axis=0, concat_axis=0, tiled=True)
    tok_recv = recv[:, :, :width_loc]
    cot_recv = recv[:, :, width_loc:]

    panel_at = jnp.clip(slot_panel, 0, column - 1)
    down_sel = jnp.take(down_col, panel_at, axis=0)
    up_sel = jnp.take(up_col, panel_at, axis=0)
    down_part = jnp.einsum("snd,srd->snr", tok_recv, down_sel, preferred_element_type=jnp.float32)
    up_part = jnp.einsum("snc,src->snr", cot_recv, up_sel, preferred_element_type=jnp.float32)
    both = lax.all_gather(
        lax.psum_scatter(jnp.stack([down_part, up_part]), "mp", scatter_dimension=1, tiled=True).astype(
            jnp.bfloat16
        ),
        "mp",
        axis=1,
        tiled=True,
    )
    down_low = both[0]
    up_grad = both[1]

    adapter_out = jnp.einsum("snr,src->snc", down_low, up_sel, preferred_element_type=jnp.float32)
    adapter_bwd = jnp.einsum("snr,srd->snd", up_grad, down_sel, preferred_element_type=jnp.float32)
    back_send = jnp.concatenate(
        [adapter_bwd.astype(jnp.bfloat16), adapter_out.astype(jnp.bfloat16)], axis=2
    )
    back = lax.all_to_all(back_send, "dx", split_axis=0, concat_axis=0, tiled=True)

    def by_panel(small, wide):
        small_p = jnp.take(small, panel_slot.reshape(-1), axis=0).reshape(column, n_x, blk, rank)
        small_p = jnp.where(panel_used[:, :, None, None], small_p, jnp.zeros_like(small_p))
        wide_p = jnp.take(wide, panel_slot.reshape(-1), axis=0)
        return (
            small_p.reshape(column, n_x * blk, rank),
            wide_p.reshape(column, n_x * blk, wide.shape[2]),
        )

    up_p, tok_p = by_panel(up_grad, tok_recv)
    grad_a_col = jnp.einsum(
        "pnr,pnd->prd", up_p, tok_p, preferred_element_type=jnp.float32
    ).reshape(column * rank, width_loc)
    low_p, cot_p = by_panel(down_low, cot_recv)
    grad_b_col = jnp.einsum(
        "pnr,pnc->prc", low_p, cot_p, preferred_element_type=jnp.float32
    ).reshape(column * rank, out_loc)
    grad_a = lax.psum_scatter(grad_a_col, "dz", scatter_dimension=0, tiled=True)
    grad_b = lax.psum_scatter(grad_b_col, "dz", scatter_dimension=0, tiled=True)
    grad_a = grad_a.astype(jnp.bfloat16).reshape(stored, rank, width_loc)
    grad_b = grad_b.astype(jnp.bfloat16).reshape(stored, rank, out_loc)

    mine_back = jnp.take(back, position, axis=0).reshape(rows, width_loc + out_loc)
    values = (base_t.T + mine_back[:, width_loc:].astype(jnp.float32)).astype(jnp.bfloat16)
    token_gradient = (base_bwd + mine_back[:, :width_loc].astype(jnp.float32)).astype(jnp.bfloat16)
    return (values, token_gradient, grad_a, grad_b)


def split_dp(mesh):
    devices = np.asarray(mesh.devices)
    n_dp, n_mp = devices.shape
    try:
        n_x = len({tuple(d.coords)[0] for d in devices[:, 0]})
    except (AttributeError, TypeError):
        n_x = 1
    if n_x < 1 or n_dp % n_x:
        n_x = 1
    return Mesh(devices.reshape(n_dp // n_x, n_x, n_mp), ("dz", "dx", "mp"))


def solution(mesh):
    in_specs = (
        P(DP, "mp"),
        P("mp", None),
        P(DP, None, "mp"),
        P(DP, None, "mp"),
        P(DP, "mp"),
        P(DP),
        P(DP),
        P(),
    )
    out_specs = (P(DP, "mp"), P(DP, "mp"), P(DP, None, "mp"), P(DP, None, "mp"))
    return jax.shard_map(
        shards, mesh=split_dp(mesh), in_specs=in_specs, out_specs=out_specs, check_vma=False
    )
```

```python
import jax
import jax.numpy as jnp
import numpy as np
from jax import lax
from jax.sharding import Mesh
from jax.sharding import PartitionSpec as P

MOST = 2
DP = ("dz", "dx")


def earlier_same(group):
    count = group.shape[-1]
    ids = jnp.arange(count, dtype=jnp.int32)
    same = (group[..., :, None] == group[..., None, :]) & (ids[:, None] > ids[None, :])
    return jnp.sum(same.astype(jnp.int32), axis=-1)


def shards(
    tokens,
    value_weight,
    adapter_down_panels,
    adapter_up_panels,
    cotangent,
    block_list_entry,
    device_tenant_list,
    tenant_location_map,
):
    rows, width_loc = tokens.shape
    stored, rank, _ = adapter_down_panels.shape
    out_loc = adapter_up_panels.shape[2]
    blocks = block_list_entry.shape[0]
    blk = rows // blocks
    n_z = lax.axis_size("dz")
    n_x = lax.axis_size("dx")
    per_x = min(MOST * n_z, blocks)
    capacity = n_x * per_x
    my_x = lax.axis_index("dx")
    column = n_z * stored

    tenant = jnp.take(device_tenant_list, block_list_entry, mode="clip")
    location = jnp.take(tenant_location_map, tenant, mode="clip")
    owner_x = (location // stored) % n_x
    position = owner_x * per_x + earlier_same(owner_x)

    slot_ids = jnp.arange(capacity, dtype=jnp.int32)
    block_ids = jnp.arange(blocks, dtype=jnp.int32)
    source = jnp.sum(
        jnp.where(position[None, :] == slot_ids[:, None], block_ids[None, :], 0), axis=1
    )

    x_location = lax.all_gather(location, "dx", axis=0, tiled=False)
    x_owner_x = (x_location // stored) % n_x
    x_rank = earlier_same(x_owner_x)
    in_column = (x_location // stored // n_x) * stored + x_location % stored
    mine = x_owner_x == my_x
    slot_panel = jnp.stack(
        [jnp.sum(jnp.where(mine & (x_rank == c), in_column + 1, 0), axis=1) for c in range(per_x)],
        axis=1,
    ).reshape(capacity) - 1
    panel_ids = jnp.arange(column, dtype=jnp.int32)
    slot_of = x_rank + (jnp.arange(n_x, dtype=jnp.int32) * per_x)[:, None]
    panel_slot = jnp.sum(
        jnp.where(
            mine[None, :, :] & (in_column[None, :, :] == panel_ids[:, None, None]),
            slot_of[None, :, :] + 1,
            0,
        ),
        axis=2,
    ) - 1
    panel_used = panel_slot >= 0
    panel_slot = jnp.clip(panel_slot, 0, capacity - 1)

    both_col = lax.all_gather(
        jnp.concatenate([adapter_down_panels, adapter_up_panels], axis=2), "dz", axis=0, tiled=True
    )
    down_col = both_col[:, :, :width_loc]
    up_col = both_col[:, :, width_loc:]

    n_mp = lax.axis_size("mp")
    base_part = lax.dot_general(
        value_weight, tokens, (((0,), (1,)), ((), ())), preferred_element_type=jnp.float32
    )

    token_blocks = tokens.reshape(blocks, blk, width_loc)
    cot_blocks = cotangent.reshape(blocks, blk, out_loc)
    send = jnp.concatenate(
        [jnp.take(token_blocks, source, axis=0), jnp.take(cot_blocks, source, axis=0)], axis=2
    )
    recv = lax.all_to_all(send, "dx", split_axis=0, concat_axis=0, tiled=True)
    tok_recv = recv[:, :, :width_loc]
    cot_recv = recv[:, :, width_loc:]

    panel_at = jnp.clip(slot_panel, 0, column - 1)
    down_sel = jnp.take(down_col, panel_at, axis=0)
    up_sel = jnp.take(up_col, panel_at, axis=0)
    down_part = jnp.einsum("snd,srd->snr", tok_recv, down_sel, preferred_element_type=jnp.float32)
    up_part = jnp.einsum("snc,src->snr", cot_recv, up_sel, preferred_element_type=jnp.float32)
    prod = jnp.stack([down_part, up_part]).reshape(2, n_mp, -1).transpose(1, 0, 2)
    prod = prod.reshape(out_loc * n_mp, -1)
    summed = lax.psum_scatter(
        jnp.concatenate([base_part, prod], axis=1), "mp", scatter_dimension=0, tiled=True
    )
    base_t = summed[:, :rows]
    prod_mine = summed[:, rows:].reshape(-1).astype(jnp.bfloat16)
    gathered = lax.all_gather(
        jnp.concatenate([cotangent.reshape(-1), prod_mine]), "mp", axis=0, tiled=False
    )
    cot_full = gathered[:, : rows * out_loc].reshape(n_mp, rows, out_loc).transpose(1, 0, 2)
    cot_full = cot_full.reshape(rows, n_mp * out_loc)
    both = gathered[:, rows * out_loc:].reshape(n_mp, 2, -1, rank).transpose(1, 0, 2, 3)
    both = both.reshape(2, capacity, blk, rank)
    down_low = both[0]
    up_grad = both[1]

    adapter_out = jnp.einsum("snr,src->snc", down_low, up_sel, preferred_element_type=jnp.float32)
    adapter_bwd = jnp.einsum("snr,srd->snd", up_grad, down_sel, preferred_element_type=jnp.float32)
    back_send = jnp.concatenate(
        [adapter_bwd.astype(jnp.bfloat16), adapter_out.astype(jnp.bfloat16)], axis=2
    )
    back = lax.all_to_all(back_send, "dx", split_axis=0, concat_axis=0, tiled=True)

    def by_panel(small, wide):
        small_p = jnp.take(small, panel_slot.reshape(-1), axis=0).reshape(column, n_x, blk, rank)
        small_p = jnp.where(panel_used[:, :, None, None], small_p, jnp.zeros_like(small_p))
        wide_p = jnp.take(wide, panel_slot.reshape(-1), axis=0)
        return (
            small_p.reshape(column, n_x * blk, rank),
            wide_p.reshape(column, n_x * blk, wide.shape[2]),
        )

    up_p, tok_p = by_panel(up_grad, tok_recv)
    grad_a_col = jnp.einsum(
        "pnr,pnd->prd", up_p, tok_p, preferred_element_type=jnp.float32
    ).reshape(column * rank, width_loc)
    low_p, cot_p = by_panel(down_low, cot_recv)
    grad_b_col = jnp.einsum(
        "pnr,pnc->prc", low_p, cot_p, preferred_element_type=jnp.float32
    ).reshape(column * rank, out_loc)
    grads = lax.psum_scatter(
        jnp.concatenate([grad_a_col, grad_b_col], axis=1), "dz", scatter_dimension=0, tiled=True
    )
    grad_a = grads[:, :width_loc]
    grad_b = grads[:, width_loc:]
    grad_a = grad_a.astype(jnp.bfloat16).reshape(stored, rank, width_loc)
    grad_b = grad_b.astype(jnp.bfloat16).reshape(stored, rank, out_loc)

    base_bwd = lax.dot_general(
        cot_full, value_weight, (((1,), (1,)), ((), ())), preferred_element_type=jnp.float32
    )
    mine_back = jnp.take(back, position, axis=0).reshape(rows, width_loc + out_loc)
    values = (base_t.T + mine_back[:, width_loc:].astype(jnp.float32)).astype(jnp.bfloat16)
    token_gradient = (base_bwd + mine_back[:, :width_loc].astype(jnp.float32)).astype(jnp.bfloat16)
    return (values, token_gradient, grad_a, grad_b)


def split_dp(mesh):
    devices = np.asarray(mesh.devices)
    n_dp, n_mp = devices.shape
    try:
        n_x = len({tuple(d.coords)[0] for d in devices[:, 0]})
    except (AttributeError, TypeError):
        n_x = 1
    if n_x < 1 or n_dp % n_x:
        n_x = 1
    return Mesh(devices.reshape(n_dp // n_x, n_x, n_mp), ("dz", "dx", "mp"))


def solution(mesh):
    in_specs = (
        P(DP, "mp"),
        P("mp", None),
        P(DP, None, "mp"),
        P(DP, None, "mp"),
        P(DP, "mp"),
        P(DP),
        P(DP),
        P(),
    )
    out_specs = (P(DP, "mp"), P(DP, "mp"), P(DP, None, "mp"), P(DP, None, "mp"))
    return jax.shard_map(
        shards, mesh=split_dp(mesh), in_specs=in_specs, out_specs=out_specs, check_vma=False
    )
```

```python
import jax
import jax.numpy as jnp
import numpy as np
from jax import lax
from jax.sharding import Mesh
from jax.sharding import PartitionSpec as P

MOST = 2
DP = ("dz", "dx")


def earlier_same(group):
    count = group.shape[-1]
    ids = jnp.arange(count, dtype=jnp.int32)
    same = (group[..., :, None] == group[..., None, :]) & (ids[:, None] > ids[None, :])
    return jnp.sum(same.astype(jnp.int32), axis=-1)


def shards(
    tokens,
    value_weight,
    adapter_down_panels,
    adapter_up_panels,
    cotangent,
    block_list_entry,
    device_tenant_list,
    tenant_location_map,
):
    rows, width_loc = tokens.shape
    stored, rank, _ = adapter_down_panels.shape
    out_loc = adapter_up_panels.shape[2]
    blocks = block_list_entry.shape[0]
    blk = rows // blocks
    n_z = lax.axis_size("dz")
    n_x = lax.axis_size("dx")
    per_x = min(MOST * n_z, blocks)
    capacity = n_x * per_x
    my_x = lax.axis_index("dx")
    column = n_z * stored

    tenant = jnp.take(device_tenant_list, block_list_entry, mode="clip")
    location = jnp.take(tenant_location_map, tenant, mode="clip")
    owner_x = (location // stored) % n_x
    position = owner_x * per_x + earlier_same(owner_x)

    slot_ids = jnp.arange(capacity, dtype=jnp.int32)
    block_ids = jnp.arange(blocks, dtype=jnp.int32)
    source = jnp.sum(
        jnp.where(position[None, :] == slot_ids[:, None], block_ids[None, :], 0), axis=1
    )

    base_part = lax.dot_general(
        value_weight, tokens, (((0,), (1,)), ((), ())), preferred_element_type=jnp.float32
    )
    location_tied, base_part = lax.optimization_barrier((location, base_part))
    x_location = lax.all_gather(location_tied, "dx", axis=0, tiled=False)
    x_owner_x = (x_location // stored) % n_x
    x_rank = earlier_same(x_owner_x)
    in_column = (x_location // stored // n_x) * stored + x_location % stored
    mine = x_owner_x == my_x
    slot_panel = jnp.stack(
        [jnp.sum(jnp.where(mine & (x_rank == c), in_column + 1, 0), axis=1) for c in range(per_x)],
        axis=1,
    ).reshape(capacity) - 1
    panel_ids = jnp.arange(column, dtype=jnp.int32)
    slot_of = x_rank + (jnp.arange(n_x, dtype=jnp.int32) * per_x)[:, None]
    panel_slot = jnp.sum(
        jnp.where(
            mine[None, :, :] & (in_column[None, :, :] == panel_ids[:, None, None]),
            slot_of[None, :, :] + 1,
            0,
        ),
        axis=2,
    ) - 1
    panel_used = panel_slot >= 0
    panel_slot = jnp.clip(panel_slot, 0, capacity - 1)

    both_col = lax.all_gather(
        jnp.concatenate([adapter_down_panels, adapter_up_panels], axis=2), "dz", axis=0, tiled=True
    )
    down_col = both_col[:, :, :width_loc]
    up_col = both_col[:, :, width_loc:]

    n_mp = lax.axis_size("mp")

    token_blocks = tokens.reshape(blocks, blk, width_loc)
    cot_blocks = cotangent.reshape(blocks, blk, out_loc)
    send = jnp.concatenate(
        [jnp.take(token_blocks, source, axis=0), jnp.take(cot_blocks, source, axis=0)], axis=2
    )
    recv = lax.all_to_all(send, "dx", split_axis=0, concat_axis=0, tiled=True)
    tok_recv = recv[:, :, :width_loc]
    cot_recv = recv[:, :, width_loc:]

    panel_at = jnp.clip(slot_panel, 0, column - 1)
    down_sel = jnp.take(down_col, panel_at, axis=0)
    up_sel = jnp.take(up_col, panel_at, axis=0)
    down_part = jnp.einsum("snd,srd->snr", tok_recv, down_sel, preferred_element_type=jnp.float32)
    up_part = jnp.einsum("snc,src->snr", cot_recv, up_sel, preferred_element_type=jnp.float32)
    prod = jnp.stack([down_part, up_part]).reshape(2, n_mp, -1).transpose(1, 0, 2)
    prod = prod.reshape(out_loc * n_mp, -1)
    summed = lax.psum_scatter(
        jnp.concatenate([base_part, prod], axis=1), "mp", scatter_dimension=0, tiled=True
    )
    base_t = summed[:, :rows]
    prod_mine = summed[:, rows:].reshape(-1).astype(jnp.bfloat16)
    gathered = lax.all_gather(
        jnp.concatenate([cotangent.reshape(-1), prod_mine]), "mp", axis=0, tiled=False
    )
    cot_parts = gathered[:, : rows * out_loc].reshape(n_mp, rows, out_loc)
    both = gathered[:, rows * out_loc:].reshape(n_mp, 2, -1, rank).transpose(1, 0, 2, 3)
    both = both.reshape(2, capacity, blk, rank)
    down_low = both[0]
    up_grad = both[1]

    adapter_out = jnp.einsum("snr,src->snc", down_low, up_sel, preferred_element_type=jnp.float32)
    adapter_bwd = jnp.einsum("snr,srd->snd", up_grad, down_sel, preferred_element_type=jnp.float32)
    back_send = jnp.concatenate(
        [adapter_bwd.astype(jnp.bfloat16), adapter_out.astype(jnp.bfloat16)], axis=2
    )
    back = lax.all_to_all(back_send, "dx", split_axis=0, concat_axis=0, tiled=True)

    def by_panel(small, wide):
        small_p = jnp.take(small, panel_slot.reshape(-1), axis=0).reshape(column, n_x, blk, rank)
        small_p = jnp.where(panel_used[:, :, None, None], small_p, jnp.zeros_like(small_p))
        wide_p = jnp.take(wide, panel_slot.reshape(-1), axis=0)
        return (
            small_p.reshape(column, n_x * blk, rank),
            wide_p.reshape(column, n_x * blk, wide.shape[2]),
        )

    up_p, tok_p = by_panel(up_grad, tok_recv)
    grad_a_col = jnp.einsum(
        "pnr,pnd->prd", up_p, tok_p, preferred_element_type=jnp.float32
    ).reshape(column * rank, width_loc)
    low_p, cot_p = by_panel(down_low, cot_recv)
    grad_b_col = jnp.einsum(
        "pnr,pnc->prc", low_p, cot_p, preferred_element_type=jnp.float32
    ).reshape(column * rank, out_loc)
    grads = lax.psum_scatter(
        jnp.concatenate([grad_a_col, grad_b_col], axis=1), "dz", scatter_dimension=0, tiled=True
    )
    grad_a = grads[:, :width_loc]
    grad_b = grads[:, width_loc:]
    grad_a = grad_a.astype(jnp.bfloat16).reshape(stored, rank, width_loc)
    grad_b = grad_b.astype(jnp.bfloat16).reshape(stored, rank, out_loc)

    base_bwd = jnp.einsum(
        "krc,dkc->rd",
        cot_parts,
        value_weight.reshape(width_loc, n_mp, out_loc),
        preferred_element_type=jnp.float32,
    )
    mine_back = jnp.take(back, position, axis=0).reshape(rows, width_loc + out_loc)
    values = (base_t.T + mine_back[:, width_loc:].astype(jnp.float32)).astype(jnp.bfloat16)
    token_gradient = (base_bwd + mine_back[:, :width_loc].astype(jnp.float32)).astype(jnp.bfloat16)
    return (values, token_gradient, grad_a, grad_b)


def split_dp(mesh):
    devices = np.asarray(mesh.devices)
    n_dp, n_mp = devices.shape
    try:
        n_x = len({tuple(d.coords)[0] for d in devices[:, 0]})
    except (AttributeError, TypeError):
        n_x = 1
    if n_x < 1 or n_dp % n_x:
        n_x = 1
    return Mesh(devices.reshape(n_dp // n_x, n_x, n_mp), ("dz", "dx", "mp"))


def solution(mesh):
    in_specs = (
        P(DP, "mp"),
        P("mp", None),
        P(DP, None, "mp"),
        P(DP, None, "mp"),
        P(DP, "mp"),
        P(DP),
        P(DP),
        P(),
    )
    out_specs = (P(DP, "mp"), P(DP, "mp"), P(DP, None, "mp"), P(DP, None, "mp"))
    return jax.shard_map(
        shards, mesh=split_dp(mesh), in_specs=in_specs, out_specs=out_specs, check_vma=False
    )
```

```python
import jax
import jax.numpy as jnp
import numpy as np
from jax import lax
from jax.sharding import Mesh
from jax.sharding import PartitionSpec as P

MOST = 2
DP = ("dz", "dx")


def earlier_same(group):
    count = group.shape[-1]
    ids = jnp.arange(count, dtype=jnp.int32)
    same = (group[..., :, None] == group[..., None, :]) & (ids[:, None] > ids[None, :])
    return jnp.sum(same.astype(jnp.int32), axis=-1)


def shards(
    tokens,
    value_weight,
    adapter_down_panels,
    adapter_up_panels,
    cotangent,
    block_list_entry,
    device_tenant_list,
    tenant_location_map,
):
    rows, width_loc = tokens.shape
    stored, rank, _ = adapter_down_panels.shape
    out_loc = adapter_up_panels.shape[2]
    blocks = block_list_entry.shape[0]
    blk = rows // blocks
    n_z = lax.axis_size("dz")
    n_x = lax.axis_size("dx")
    per_x = min(MOST * n_z, blocks)
    capacity = n_x * per_x
    my_x = lax.axis_index("dx")
    column = n_z * stored

    tenant = jnp.take(device_tenant_list, block_list_entry, mode="clip")
    location = jnp.take(tenant_location_map, tenant, mode="clip")
    owner_x = (location // stored) % n_x
    position = owner_x * per_x + earlier_same(owner_x)

    slot_ids = jnp.arange(capacity, dtype=jnp.int32)
    block_ids = jnp.arange(blocks, dtype=jnp.int32)
    source = jnp.sum(
        jnp.where(position[None, :] == slot_ids[:, None], block_ids[None, :], 0), axis=1
    )

    base_part = lax.dot_general(
        value_weight, tokens, (((0,), (1,)), ((), ())), preferred_element_type=jnp.float32
    )
    location_tied, base_part = lax.optimization_barrier((location, base_part))
    base_t = lax.psum_scatter(base_part, "mp", scatter_dimension=0, tiled=True)
    x_location = lax.all_gather(location_tied, "dx", axis=0, tiled=False)
    x_owner_x = (x_location // stored) % n_x
    x_rank = earlier_same(x_owner_x)
    in_column = (x_location // stored // n_x) * stored + x_location % stored
    mine = x_owner_x == my_x
    slot_panel = jnp.stack(
        [jnp.sum(jnp.where(mine & (x_rank == c), in_column + 1, 0), axis=1) for c in range(per_x)],
        axis=1,
    ).reshape(capacity) - 1
    panel_ids = jnp.arange(column, dtype=jnp.int32)
    slot_of = x_rank + (jnp.arange(n_x, dtype=jnp.int32) * per_x)[:, None]
    panel_slot = jnp.sum(
        jnp.where(
            mine[None, :, :] & (in_column[None, :, :] == panel_ids[:, None, None]),
            slot_of[None, :, :] + 1,
            0,
        ),
        axis=2,
    ) - 1
    panel_used = panel_slot >= 0
    panel_slot = jnp.clip(panel_slot, 0, capacity - 1)

    both_col = lax.all_gather(
        jnp.concatenate([adapter_down_panels, adapter_up_panels], axis=2), "dz", axis=0, tiled=True
    )
    down_col = both_col[:, :, :width_loc]
    up_col = both_col[:, :, width_loc:]

    n_mp = lax.axis_size("mp")

    token_blocks = tokens.reshape(blocks, blk, width_loc)
    cot_blocks = cotangent.reshape(blocks, blk, out_loc)
    send = jnp.concatenate(
        [jnp.take(token_blocks, source, axis=0), jnp.take(cot_blocks, source, axis=0)], axis=2
    )
    recv = lax.all_to_all(send, "dx", split_axis=0, concat_axis=0, tiled=True)
    tok_recv = recv[:, :, :width_loc]
    cot_recv = recv[:, :, width_loc:]

    panel_at = jnp.clip(slot_panel, 0, column - 1)
    down_sel = jnp.take(down_col, panel_at, axis=0)
    up_sel = jnp.take(up_col, panel_at, axis=0)
    down_part = jnp.einsum("snd,srd->snr", tok_recv, down_sel, preferred_element_type=jnp.float32)
    up_part = jnp.einsum("snc,src->snr", cot_recv, up_sel, preferred_element_type=jnp.float32)
    prod = jnp.stack([down_part, up_part]).reshape(2, n_mp, -1).transpose(1, 0, 2)
    prod = prod.reshape(out_loc * n_mp, -1)
    summed = lax.psum_scatter(prod, "mp", scatter_dimension=0, tiled=True)
    prod_mine = summed.reshape(-1).astype(jnp.bfloat16)
    gathered = lax.all_gather(
        jnp.concatenate([cotangent.reshape(-1), prod_mine]), "mp", axis=0, tiled=False
    )
    cot_parts = gathered[:, : rows * out_loc].reshape(n_mp, rows, out_loc)
    both = gathered[:, rows * out_loc:].reshape(n_mp, 2, -1, rank).transpose(1, 0, 2, 3)
    both = both.reshape(2, capacity, blk, rank)
    down_low = both[0]
    up_grad = both[1]

    adapter_out = jnp.einsum("snr,src->snc", down_low, up_sel, preferred_element_type=jnp.float32)
    adapter_bwd = jnp.einsum("snr,srd->snd", up_grad, down_sel, preferred_element_type=jnp.float32)
    back_send = jnp.concatenate(
        [adapter_bwd.astype(jnp.bfloat16), adapter_out.astype(jnp.bfloat16)], axis=2
    )
    back = lax.all_to_all(back_send, "dx", split_axis=0, concat_axis=0, tiled=True)

    def by_panel(small, wide):
        small_p = jnp.take(small, panel_slot.reshape(-1), axis=0).reshape(column, n_x, blk, rank)
        small_p = jnp.where(panel_used[:, :, None, None], small_p, jnp.zeros_like(small_p))
        wide_p = jnp.take(wide, panel_slot.reshape(-1), axis=0)
        return (
            small_p.reshape(column, n_x * blk, rank),
            wide_p.reshape(column, n_x * blk, wide.shape[2]),
        )

    up_p, tok_p = by_panel(up_grad, tok_recv)
    grad_a_col = jnp.einsum(
        "pnr,pnd->prd", up_p, tok_p, preferred_element_type=jnp.float32
    ).reshape(column * rank, width_loc)
    low_p, cot_p = by_panel(down_low, cot_recv)
    grad_b_col = jnp.einsum(
        "pnr,pnc->prc", low_p, cot_p, preferred_element_type=jnp.float32
    ).reshape(column * rank, out_loc)
    grads = lax.psum_scatter(
        jnp.concatenate([grad_a_col, grad_b_col], axis=1), "dz", scatter_dimension=0, tiled=True
    )
    grad_a = grads[:, :width_loc]
    grad_b = grads[:, width_loc:]
    grad_a = grad_a.astype(jnp.bfloat16).reshape(stored, rank, width_loc)
    grad_b = grad_b.astype(jnp.bfloat16).reshape(stored, rank, out_loc)

    base_bwd = jnp.einsum(
        "krc,dkc->rd",
        cot_parts,
        value_weight.reshape(width_loc, n_mp, out_loc),
        preferred_element_type=jnp.float32,
    )
    mine_back = jnp.take(back, position, axis=0).reshape(rows, width_loc + out_loc)
    values = (base_t.T + mine_back[:, width_loc:].astype(jnp.float32)).astype(jnp.bfloat16)
    token_gradient = (base_bwd + mine_back[:, :width_loc].astype(jnp.float32)).astype(jnp.bfloat16)
    return (values, token_gradient, grad_a, grad_b)


def split_dp(mesh):
    devices = np.asarray(mesh.devices)
    n_dp, n_mp = devices.shape
    try:
        n_x = len({tuple(d.coords)[0] for d in devices[:, 0]})
    except (AttributeError, TypeError):
        n_x = 1
    if n_x < 1 or n_dp % n_x:
        n_x = 1
    return Mesh(devices.reshape(n_dp // n_x, n_x, n_mp), ("dz", "dx", "mp"))


def solution(mesh):
    in_specs = (
        P(DP, "mp"),
        P("mp", None),
        P(DP, None, "mp"),
        P(DP, None, "mp"),
        P(DP, "mp"),
        P(DP),
        P(DP),
        P(),
    )
    out_specs = (P(DP, "mp"), P(DP, "mp"), P(DP, None, "mp"), P(DP, None, "mp"))
    return jax.shard_map(
        shards, mesh=split_dp(mesh), in_specs=in_specs, out_specs=out_specs, check_vma=False
    )
```

```python
import jax
import jax.numpy as jnp
import numpy as np
from jax import lax
from jax.sharding import Mesh
from jax.sharding import PartitionSpec as P

MOST = 2
DP = ("dz", "dx")


def earlier_same(group):
    count = group.shape[-1]
    ids = jnp.arange(count, dtype=jnp.int32)
    same = (group[..., :, None] == group[..., None, :]) & (ids[:, None] > ids[None, :])
    return jnp.sum(same.astype(jnp.int32), axis=-1)


def shards(
    tokens,
    value_weight,
    adapter_down_panels,
    adapter_up_panels,
    cotangent,
    block_list_entry,
    device_tenant_list,
    tenant_location_map,
):
    rows, width_loc = tokens.shape
    stored, rank, _ = adapter_down_panels.shape
    out_loc = adapter_up_panels.shape[2]
    blocks = block_list_entry.shape[0]
    blk = rows // blocks
    n_z = lax.axis_size("dz")
    n_x = lax.axis_size("dx")
    per_x = min(MOST * n_z, blocks)
    capacity = n_x * per_x
    my_x = lax.axis_index("dx")
    column = n_z * stored

    tenant = jnp.take(device_tenant_list, block_list_entry, mode="clip")
    location = jnp.take(tenant_location_map, tenant, mode="clip")
    owner_x = (location // stored) % n_x
    position = owner_x * per_x + earlier_same(owner_x)

    slot_ids = jnp.arange(capacity, dtype=jnp.int32)
    block_ids = jnp.arange(blocks, dtype=jnp.int32)
    source = jnp.sum(
        jnp.where(position[None, :] == slot_ids[:, None], block_ids[None, :], 0), axis=1
    )

    base_part = lax.dot_general(
        value_weight, tokens, (((0,), (1,)), ((), ())), preferred_element_type=jnp.float32
    )
    location_tied, base_part = lax.optimization_barrier((location, base_part))
    base_t = lax.psum_scatter(base_part, "mp", scatter_dimension=0, tiled=True)
    x_location = lax.all_gather(location_tied, "dx", axis=0, tiled=False)
    x_owner_x = (x_location // stored) % n_x
    x_rank = earlier_same(x_owner_x)
    in_column = (x_location // stored // n_x) * stored + x_location % stored
    mine = x_owner_x == my_x
    slot_panel = jnp.stack(
        [jnp.sum(jnp.where(mine & (x_rank == c), in_column + 1, 0), axis=1) for c in range(per_x)],
        axis=1,
    ).reshape(capacity) - 1
    panel_ids = jnp.arange(column, dtype=jnp.int32)
    slot_of = x_rank + (jnp.arange(n_x, dtype=jnp.int32) * per_x)[:, None]
    panel_slot = jnp.sum(
        jnp.where(
            mine[None, :, :] & (in_column[None, :, :] == panel_ids[:, None, None]),
            slot_of[None, :, :] + 1,
            0,
        ),
        axis=2,
    ) - 1
    panel_used = panel_slot >= 0
    panel_slot = jnp.clip(panel_slot, 0, capacity - 1)

    both_col = lax.all_gather(
        jnp.concatenate([adapter_down_panels, adapter_up_panels], axis=2), "dz", axis=0, tiled=True
    )
    down_col = both_col[:, :, :width_loc]
    up_col = both_col[:, :, width_loc:]

    n_mp = lax.axis_size("mp")

    token_blocks = tokens.reshape(blocks, blk, width_loc)
    cot_blocks = cotangent.reshape(blocks, blk, out_loc)
    send = jnp.concatenate(
        [jnp.take(token_blocks, source, axis=0), jnp.take(cot_blocks, source, axis=0)], axis=2
    )
    recv = lax.all_to_all(send, "dx", split_axis=0, concat_axis=0, tiled=True)
    tok_recv = recv[:, :, :width_loc]
    cot_recv = recv[:, :, width_loc:]

    panel_at = jnp.clip(slot_panel, 0, column - 1)
    down_sel = jnp.take(down_col, panel_at, axis=0)
    up_sel = jnp.take(up_col, panel_at, axis=0)
    down_part = jnp.einsum("snd,srd->snr", tok_recv, down_sel, preferred_element_type=jnp.float32)
    up_part = jnp.einsum("snc,src->snr", cot_recv, up_sel, preferred_element_type=jnp.float32)
    both = lax.psum(jnp.stack([down_part, up_part]), "mp").astype(jnp.bfloat16)
    cot_parts = lax.all_gather(cotangent, "mp", axis=0, tiled=False)
    down_low = both[0]
    up_grad = both[1]

    adapter_out = jnp.einsum("snr,src->snc", down_low, up_sel, preferred_element_type=jnp.float32)
    adapter_bwd = jnp.einsum("snr,srd->snd", up_grad, down_sel, preferred_element_type=jnp.float32)
    back_send = jnp.concatenate(
        [adapter_bwd.astype(jnp.bfloat16), adapter_out.astype(jnp.bfloat16)], axis=2
    )
    back = lax.all_to_all(back_send, "dx", split_axis=0, concat_axis=0, tiled=True)

    def by_panel(small, wide):
        small_p = jnp.take(small, panel_slot.reshape(-1), axis=0).reshape(column, n_x, blk, rank)
        small_p = jnp.where(panel_used[:, :, None, None], small_p, jnp.zeros_like(small_p))
        wide_p = jnp.take(wide, panel_slot.reshape(-1), axis=0)
        return (
            small_p.reshape(column, n_x * blk, rank),
            wide_p.reshape(column, n_x * blk, wide.shape[2]),
        )

    up_p, tok_p = by_panel(up_grad, tok_recv)
    grad_a_col = jnp.einsum(
        "pnr,pnd->prd", up_p, tok_p, preferred_element_type=jnp.float32
    ).reshape(column * rank, width_loc)
    low_p, cot_p = by_panel(down_low, cot_recv)
    grad_b_col = jnp.einsum(
        "pnr,pnc->prc", low_p, cot_p, preferred_element_type=jnp.float32
    ).reshape(column * rank, out_loc)
    grads = lax.psum_scatter(
        jnp.concatenate([grad_a_col, grad_b_col], axis=1), "dz", scatter_dimension=0, tiled=True
    )
    grad_a = grads[:, :width_loc]
    grad_b = grads[:, width_loc:]
    grad_a = grad_a.astype(jnp.bfloat16).reshape(stored, rank, width_loc)
    grad_b = grad_b.astype(jnp.bfloat16).reshape(stored, rank, out_loc)

    base_bwd = jnp.einsum(
        "krc,dkc->rd",
        cot_parts,
        value_weight.reshape(width_loc, n_mp, out_loc),
        preferred_element_type=jnp.float32,
    )
    mine_back = jnp.take(back, position, axis=0).reshape(rows, width_loc + out_loc)
    values = (base_t.T + mine_back[:, width_loc:].astype(jnp.float32)).astype(jnp.bfloat16)
    token_gradient = (base_bwd + mine_back[:, :width_loc].astype(jnp.float32)).astype(jnp.bfloat16)
    return (values, token_gradient, grad_a, grad_b)


def split_dp(mesh):
    devices = np.asarray(mesh.devices)
    n_dp, n_mp = devices.shape
    try:
        n_x = len({tuple(d.coords)[0] for d in devices[:, 0]})
    except (AttributeError, TypeError):
        n_x = 1
    if n_x < 1 or n_dp % n_x:
        n_x = 1
    return Mesh(devices.reshape(n_dp // n_x, n_x, n_mp), ("dz", "dx", "mp"))


def solution(mesh):
    in_specs = (
        P(DP, "mp"),
        P("mp", None),
        P(DP, None, "mp"),
        P(DP, None, "mp"),
        P(DP, "mp"),
        P(DP),
        P(DP),
        P(),
    )
    out_specs = (P(DP, "mp"), P(DP, "mp"), P(DP, None, "mp"), P(DP, None, "mp"))
    return jax.shard_map(
        shards, mesh=split_dp(mesh), in_specs=in_specs, out_specs=out_specs, check_vma=False
    )
```

```python
import jax
import jax.numpy as jnp
import numpy as np
from jax import lax
from jax.sharding import Mesh
from jax.sharding import PartitionSpec as P

MOST = 2
DP = ("dz", "dx")


def earlier_same(group):
    count = group.shape[-1]
    ids = jnp.arange(count, dtype=jnp.int32)
    same = (group[..., :, None] == group[..., None, :]) & (ids[:, None] > ids[None, :])
    return jnp.sum(same.astype(jnp.int32), axis=-1)


def shards(
    tokens,
    value_weight,
    adapter_down_panels,
    adapter_up_panels,
    cotangent,
    block_list_entry,
    device_tenant_list,
    tenant_location_map,
):
    rows, width_loc = tokens.shape
    stored, rank, _ = adapter_down_panels.shape
    out_loc = adapter_up_panels.shape[2]
    blocks = block_list_entry.shape[0]
    blk = rows // blocks
    n_z = lax.axis_size("dz")
    n_x = lax.axis_size("dx")
    per_x = min(MOST * n_z, blocks)
    capacity = n_x * per_x
    my_x = lax.axis_index("dx")
    column = n_z * stored

    tenant = jnp.take(device_tenant_list, block_list_entry, mode="clip")
    location = jnp.take(tenant_location_map, tenant, mode="clip")
    owner_x = (location // stored) % n_x
    position = jnp.clip(owner_x * per_x + earlier_same(owner_x), 0, capacity - 1)

    slot_ids = jnp.arange(capacity, dtype=jnp.int32)
    block_ids = jnp.arange(blocks, dtype=jnp.int32)
    source = jnp.sum(
        jnp.where(position[None, :] == slot_ids[:, None], block_ids[None, :], 0), axis=1
    )

    base_part = lax.dot_general(
        value_weight, tokens, (((0,), (1,)), ((), ())), preferred_element_type=jnp.float32
    )
    location_tied, base_part = lax.optimization_barrier((location, base_part))
    base_t = lax.psum_scatter(base_part, "mp", scatter_dimension=0, tiled=True)
    x_location = lax.all_gather(location_tied, "dx", axis=0, tiled=False)
    x_owner_x = (x_location // stored) % n_x
    x_rank = earlier_same(x_owner_x)
    in_column = (x_location // stored // n_x) * stored + x_location % stored
    mine = x_owner_x == my_x
    slot_panel = jnp.stack(
        [jnp.sum(jnp.where(mine & (x_rank == c), in_column + 1, 0), axis=1) for c in range(per_x)],
        axis=1,
    ).reshape(capacity) - 1
    panel_ids = jnp.arange(column, dtype=jnp.int32)
    slot_of = x_rank + (jnp.arange(n_x, dtype=jnp.int32) * per_x)[:, None]
    panel_slot = jnp.sum(
        jnp.where(
            mine[None, :, :] & (in_column[None, :, :] == panel_ids[:, None, None]),
            slot_of[None, :, :] + 1,
            0,
        ),
        axis=2,
    ) - 1
    panel_used = panel_slot >= 0
    panel_slot = jnp.clip(panel_slot, 0, capacity - 1)

    both_col = lax.all_gather(
        jnp.concatenate([adapter_down_panels, adapter_up_panels], axis=2), "dz", axis=0, tiled=True
    )
    down_col = both_col[:, :, :width_loc]
    up_col = both_col[:, :, width_loc:]

    n_mp = lax.axis_size("mp")

    token_blocks = tokens.reshape(blocks, blk, width_loc)
    cot_blocks = cotangent.reshape(blocks, blk, out_loc)
    send = jnp.concatenate(
        [jnp.take(token_blocks, source, axis=0, mode="clip"), jnp.take(cot_blocks, source, axis=0, mode="clip")], axis=2
    )
    recv = lax.all_to_all(send, "dx", split_axis=0, concat_axis=0, tiled=True)
    tok_recv = recv[:, :, :width_loc]
    cot_recv = recv[:, :, width_loc:]

    panel_at = jnp.clip(slot_panel, 0, column - 1)
    down_sel = jnp.take(down_col, panel_at, axis=0, mode="clip")
    up_sel = jnp.take(up_col, panel_at, axis=0, mode="clip")
    down_part = jnp.einsum("snd,srd->snr", tok_recv, down_sel, preferred_element_type=jnp.float32)
    up_part = jnp.einsum("snc,src->snr", cot_recv, up_sel, preferred_element_type=jnp.float32)
    both = lax.psum(jnp.stack([down_part, up_part]), "mp").astype(jnp.bfloat16)
    cot_parts = lax.all_gather(cotangent, "mp", axis=0, tiled=False)
    down_low = both[0]
    up_grad = both[1]

    adapter_out = jnp.einsum("snr,src->snc", down_low, up_sel, preferred_element_type=jnp.float32)
    adapter_bwd = jnp.einsum("snr,srd->snd", up_grad, down_sel, preferred_element_type=jnp.float32)
    back_send = jnp.concatenate(
        [adapter_bwd.astype(jnp.bfloat16), adapter_out.astype(jnp.bfloat16)], axis=2
    )
    back = lax.all_to_all(back_send, "dx", split_axis=0, concat_axis=0, tiled=True)

    def by_panel(small, wide):
        small_p = jnp.take(small, panel_slot.reshape(-1), axis=0, mode="clip").reshape(column, n_x, blk, rank)
        small_p = jnp.where(panel_used[:, :, None, None], small_p, jnp.zeros_like(small_p))
        wide_p = jnp.take(wide, panel_slot.reshape(-1), axis=0, mode="clip")
        return (
            small_p.reshape(column, n_x * blk, rank),
            wide_p.reshape(column, n_x * blk, wide.shape[2]),
        )

    up_p, tok_p = by_panel(up_grad, tok_recv)
    grad_a_col = jnp.einsum(
        "pnr,pnd->prd", up_p, tok_p, preferred_element_type=jnp.float32
    ).reshape(column * rank, width_loc)
    low_p, cot_p = by_panel(down_low, cot_recv)
    grad_b_col = jnp.einsum(
        "pnr,pnc->prc", low_p, cot_p, preferred_element_type=jnp.float32
    ).reshape(column * rank, out_loc)
    grads = lax.psum_scatter(
        jnp.concatenate([grad_a_col, grad_b_col], axis=1), "dz", scatter_dimension=0, tiled=True
    )
    grad_a = grads[:, :width_loc]
    grad_b = grads[:, width_loc:]
    grad_a = grad_a.astype(jnp.bfloat16).reshape(stored, rank, width_loc)
    grad_b = grad_b.astype(jnp.bfloat16).reshape(stored, rank, out_loc)

    base_bwd = jnp.einsum(
        "krc,dkc->rd",
        cot_parts,
        value_weight.reshape(width_loc, n_mp, out_loc),
        preferred_element_type=jnp.float32,
    )
    mine_back = jnp.take(back, position, axis=0, mode="clip").reshape(rows, width_loc + out_loc)
    values = (base_t.T + mine_back[:, width_loc:].astype(jnp.float32)).astype(jnp.bfloat16)
    token_gradient = (base_bwd + mine_back[:, :width_loc].astype(jnp.float32)).astype(jnp.bfloat16)
    return (values, token_gradient, grad_a, grad_b)


def split_dp(mesh):
    devices = np.asarray(mesh.devices)
    n_dp, n_mp = devices.shape
    try:
        n_x = len({tuple(d.coords)[0] for d in devices[:, 0]})
    except (AttributeError, TypeError):
        n_x = 1
    if n_x < 1 or n_dp % n_x:
        n_x = 1
    return Mesh(devices.reshape(n_dp // n_x, n_x, n_mp), ("dz", "dx", "mp"))


def solution(mesh):
    in_specs = (
        P(DP, "mp"),
        P("mp", None),
        P(DP, None, "mp"),
        P(DP, None, "mp"),
        P(DP, "mp"),
        P(DP),
        P(DP),
        P(),
    )
    out_specs = (P(DP, "mp"), P(DP, "mp"), P(DP, None, "mp"), P(DP, None, "mp"))
    return jax.shard_map(
        shards, mesh=split_dp(mesh), in_specs=in_specs, out_specs=out_specs, check_vma=False
    )
```

```python
import jax
import jax.numpy as jnp
import numpy as np
from jax import lax
from jax.sharding import Mesh
from jax.sharding import PartitionSpec as P

MOST = 2
DP = ("dz", "dx")


def earlier_same(group):
    count = group.shape[-1]
    ids = jnp.arange(count, dtype=jnp.int32)
    same = (group[..., :, None] == group[..., None, :]) & (ids[:, None] > ids[None, :])
    return jnp.sum(same.astype(jnp.int32), axis=-1)


def shards(
    tokens,
    value_weight,
    adapter_down_panels,
    adapter_up_panels,
    cotangent,
    block_list_entry,
    device_tenant_list,
    tenant_location_map,
):
    rows, width_loc = tokens.shape
    stored, rank, _ = adapter_down_panels.shape
    out_loc = adapter_up_panels.shape[2]
    blocks = block_list_entry.shape[0]
    blk = rows // blocks
    n_z = lax.axis_size("dz")
    n_x = lax.axis_size("dx")
    per_x = min(MOST * n_z, blocks)
    capacity = n_x * per_x
    my_x = lax.axis_index("dx")
    column = n_z * stored

    tenant = jnp.take(device_tenant_list, block_list_entry, mode="clip")
    location = jnp.take(tenant_location_map, tenant, mode="clip")
    owner_x = (location // stored) % n_x
    position = jnp.clip(owner_x * per_x + earlier_same(owner_x), 0, capacity - 1)

    slot_ids = jnp.arange(capacity, dtype=jnp.int32)
    block_ids = jnp.arange(blocks, dtype=jnp.int32)
    source = jnp.sum(
        jnp.where(position[None, :] == slot_ids[:, None], block_ids[None, :], 0), axis=1
    )

    base_part = lax.dot_general(
        value_weight, tokens, (((0,), (1,)), ((), ())), preferred_element_type=jnp.float32
    )
    location_tied, base_part = lax.optimization_barrier((location, base_part))
    base_t = lax.psum_scatter(base_part, "mp", scatter_dimension=0, tiled=True)
    x_location = lax.all_gather(location_tied, "dx", axis=0, tiled=False)
    x_owner_x = (x_location // stored) % n_x
    x_rank = earlier_same(x_owner_x)
    in_column = (x_location // stored // n_x) * stored + x_location % stored
    mine = x_owner_x == my_x
    slot_panel = jnp.stack(
        [jnp.sum(jnp.where(mine & (x_rank == c), in_column + 1, 0), axis=1) for c in range(per_x)],
        axis=1,
    ).reshape(capacity) - 1
    panel_ids = jnp.arange(column, dtype=jnp.int32)
    slot_of = x_rank + (jnp.arange(n_x, dtype=jnp.int32) * per_x)[:, None]
    panel_slot = jnp.sum(
        jnp.where(
            mine[None, :, :] & (in_column[None, :, :] == panel_ids[:, None, None]),
            slot_of[None, :, :] + 1,
            0,
        ),
        axis=2,
    ) - 1
    panel_used = panel_slot >= 0
    panel_slot = jnp.clip(panel_slot, 0, capacity - 1)

    both_col = lax.all_gather(
        jnp.concatenate([adapter_down_panels, adapter_up_panels], axis=2), "dz", axis=0, tiled=True
    )
    down_col = both_col[:, :, :width_loc]
    up_col = both_col[:, :, width_loc:]

    n_mp = lax.axis_size("mp")

    token_blocks = tokens.reshape(blocks, blk, width_loc)
    cot_blocks = cotangent.reshape(blocks, blk, out_loc)
    send = jnp.concatenate(
        [jnp.take(token_blocks, source, axis=0, mode="clip"), jnp.take(cot_blocks, source, axis=0, mode="clip")], axis=2
    )
    recv = lax.all_to_all(send, "dx", split_axis=0, concat_axis=0, tiled=True)
    tok_recv = recv[:, :, :width_loc]
    cot_recv = recv[:, :, width_loc:]

    panel_at = jnp.clip(slot_panel, 0, column - 1)
    down_sel = jnp.take(down_col, panel_at, axis=0, mode="clip")
    up_sel = jnp.take(up_col, panel_at, axis=0, mode="clip")
    down_part = jnp.einsum("snd,srd->snr", tok_recv, down_sel, preferred_element_type=jnp.float32)
    up_part = jnp.einsum("snc,src->snr", cot_recv, up_sel, preferred_element_type=jnp.float32)
    both = lax.psum(jnp.stack([down_part, up_part]), "mp").astype(jnp.bfloat16)
    cot_parts = lax.all_gather(cotangent, "mp", axis=0, tiled=False)
    down_low = both[0]
    up_grad = both[1]

    adapter_out = jnp.einsum("snr,src->snc", down_low, up_sel, preferred_element_type=jnp.float32)
    adapter_bwd = jnp.einsum("snr,srd->snd", up_grad, down_sel, preferred_element_type=jnp.float32)
    back_send = jnp.concatenate(
        [adapter_bwd.astype(jnp.bfloat16), adapter_out.astype(jnp.bfloat16)], axis=2
    )
    back = lax.all_to_all(back_send, "dx", split_axis=0, concat_axis=0, tiled=True)

    def by_panel(small):
        small_p = jnp.take(small, panel_slot.reshape(-1), axis=0, mode="clip").reshape(column, n_x, blk, rank)
        small_p = jnp.where(panel_used[:, :, None, None], small_p, jnp.zeros_like(small_p))
        return small_p.reshape(column, n_x * blk, rank)

    rows_p = jnp.take(recv, panel_slot.reshape(-1), axis=0, mode="clip").reshape(
        column, n_x * blk, width_loc + out_loc
    )
    grad_up = jnp.einsum("pnr,pnd->prd", by_panel(up_grad), rows_p, preferred_element_type=jnp.float32)
    grad_low = jnp.einsum("pnr,pnd->prd", by_panel(down_low), rows_p, preferred_element_type=jnp.float32)
    feature = jnp.arange(width_loc + out_loc, dtype=jnp.int32)[None, None, :]
    grads_col = jnp.where(feature < width_loc, grad_up, grad_low)
    grads = lax.psum_scatter(
        grads_col.reshape(column * rank, width_loc + out_loc), "dz", scatter_dimension=0, tiled=True
    )
    grad_a = grads[:, :width_loc]
    grad_b = grads[:, width_loc:]
    grad_a = grad_a.astype(jnp.bfloat16).reshape(stored, rank, width_loc)
    grad_b = grad_b.astype(jnp.bfloat16).reshape(stored, rank, out_loc)

    base_bwd = jnp.einsum(
        "krc,dkc->rd",
        cot_parts,
        value_weight.reshape(width_loc, n_mp, out_loc),
        preferred_element_type=jnp.float32,
    )
    mine_back = jnp.take(back, position, axis=0, mode="clip").reshape(rows, width_loc + out_loc)
    values = (base_t.T + mine_back[:, width_loc:].astype(jnp.float32)).astype(jnp.bfloat16)
    token_gradient = (base_bwd + mine_back[:, :width_loc].astype(jnp.float32)).astype(jnp.bfloat16)
    return (values, token_gradient, grad_a, grad_b)


def split_dp(mesh):
    devices = np.asarray(mesh.devices)
    n_dp, n_mp = devices.shape
    try:
        n_x = len({tuple(d.coords)[0] for d in devices[:, 0]})
    except (AttributeError, TypeError):
        n_x = 1
    if n_x < 1 or n_dp % n_x:
        n_x = 1
    return Mesh(devices.reshape(n_dp // n_x, n_x, n_mp), ("dz", "dx", "mp"))


def solution(mesh):
    in_specs = (
        P(DP, "mp"),
        P("mp", None),
        P(DP, None, "mp"),
        P(DP, None, "mp"),
        P(DP, "mp"),
        P(DP),
        P(DP),
        P(),
    )
    out_specs = (P(DP, "mp"), P(DP, "mp"), P(DP, None, "mp"), P(DP, None, "mp"))
    return jax.shard_map(
        shards, mesh=split_dp(mesh), in_specs=in_specs, out_specs=out_specs, check_vma=False
    )
```

```python
import jax
import jax.numpy as jnp
import numpy as np
from jax import lax
from jax.sharding import Mesh
from jax.sharding import PartitionSpec as P

MOST = 2
DP = ("dz", "dx")


def earlier_same(group):
    count = group.shape[-1]
    ids = jnp.arange(count, dtype=jnp.int32)
    same = (group[..., :, None] == group[..., None, :]) & (ids[:, None] > ids[None, :])
    return jnp.sum(same.astype(jnp.int32), axis=-1)


def shards(
    tokens,
    value_weight,
    adapter_down_panels,
    adapter_up_panels,
    cotangent,
    block_list_entry,
    device_tenant_list,
    tenant_location_map,
):
    rows, width_loc = tokens.shape
    stored, rank, _ = adapter_down_panels.shape
    out_loc = adapter_up_panels.shape[2]
    blocks = block_list_entry.shape[0]
    blk = rows // blocks
    n_z = lax.axis_size("dz")
    n_x = lax.axis_size("dx")
    per_x = min(MOST * n_z, blocks)
    capacity = n_x * per_x
    my_x = lax.axis_index("dx")
    column = n_z * stored

    tenant = jnp.take(device_tenant_list, block_list_entry, mode="clip")
    location = jnp.take(tenant_location_map, tenant, mode="clip")
    owner_x = (location // stored) % n_x
    position = jnp.clip(owner_x * per_x + earlier_same(owner_x), 0, capacity - 1)

    slot_ids = jnp.arange(capacity, dtype=jnp.int32)
    block_ids = jnp.arange(blocks, dtype=jnp.int32)
    source = jnp.sum(
        jnp.where(position[None, :] == slot_ids[:, None], block_ids[None, :], 0), axis=1
    )

    base_part = lax.dot_general(
        value_weight, tokens, (((0,), (1,)), ((), ())), preferred_element_type=jnp.float32
    )
    location_tied, base_part = lax.optimization_barrier((location, base_part))
    base_t = lax.psum_scatter(base_part, "mp", scatter_dimension=0, tiled=True)
    x_location = lax.all_gather(location_tied, "dx", axis=0, tiled=False)
    x_owner_x = (x_location // stored) % n_x
    x_rank = earlier_same(x_owner_x)
    in_column = (x_location // stored // n_x) * stored + x_location % stored
    mine = x_owner_x == my_x
    slot_panel = jnp.stack(
        [jnp.sum(jnp.where(mine & (x_rank == c), in_column + 1, 0), axis=1) for c in range(per_x)],
        axis=1,
    ).reshape(capacity) - 1
    panel_ids = jnp.arange(column, dtype=jnp.int32)
    slot_of = x_rank + (jnp.arange(n_x, dtype=jnp.int32) * per_x)[:, None]
    panel_slot = jnp.sum(
        jnp.where(
            mine[None, :, :] & (in_column[None, :, :] == panel_ids[:, None, None]),
            slot_of[None, :, :] + 1,
            0,
        ),
        axis=2,
    ) - 1
    panel_used = panel_slot >= 0
    panel_slot = jnp.clip(panel_slot, 0, capacity - 1)

    both_col = lax.all_gather(
        jnp.concatenate([adapter_down_panels, adapter_up_panels], axis=2), "dz", axis=0, tiled=True
    )
    down_col = both_col[:, :, :width_loc]
    up_col = both_col[:, :, width_loc:]

    n_mp = lax.axis_size("mp")

    token_blocks = tokens.reshape(blocks, blk, width_loc)
    cot_blocks = cotangent.reshape(blocks, blk, out_loc)
    send = jnp.concatenate(
        [jnp.take(token_blocks, source, axis=0, mode="clip"), jnp.take(cot_blocks, source, axis=0, mode="clip")], axis=2
    )
    recv = lax.all_to_all(send, "dx", split_axis=0, concat_axis=0, tiled=True)
    width_all = width_loc + out_loc
    feature = jnp.arange(width_all, dtype=jnp.int32)[None, None, :]
    panel_at = jnp.clip(slot_panel, 0, column - 1)
    sel = jnp.take(both_col, panel_at, axis=0, mode="clip")
    down_sel = jnp.where(feature < width_loc, sel, jnp.zeros_like(sel))
    up_sel = jnp.where(feature >= width_loc, sel, jnp.zeros_like(sel))
    down_part = jnp.einsum("snd,srd->snr", recv, down_sel, preferred_element_type=jnp.float32)
    up_part = jnp.einsum("snd,srd->snr", recv, up_sel, preferred_element_type=jnp.float32)
    both = lax.psum(jnp.stack([down_part, up_part]), "mp").astype(jnp.bfloat16)
    cot_parts = lax.all_gather(cotangent, "mp", axis=0, tiled=False)
    down_low = both[0]
    up_grad = both[1]

    back_send = (
        jnp.einsum("snr,srd->snd", up_grad, down_sel, preferred_element_type=jnp.float32)
        + jnp.einsum("snr,srd->snd", down_low, up_sel, preferred_element_type=jnp.float32)
    ).astype(jnp.bfloat16)
    back = lax.all_to_all(back_send, "dx", split_axis=0, concat_axis=0, tiled=True)

    def by_panel(small):
        small_p = jnp.take(small, panel_slot.reshape(-1), axis=0, mode="clip").reshape(column, n_x, blk, rank)
        small_p = jnp.where(panel_used[:, :, None, None], small_p, jnp.zeros_like(small_p))
        return small_p.reshape(column, n_x * blk, rank)

    rows_p = jnp.take(recv, panel_slot.reshape(-1), axis=0, mode="clip").reshape(
        column, n_x * blk, width_loc + out_loc
    )
    grad_up = jnp.einsum("pnr,pnd->prd", by_panel(up_grad), rows_p, preferred_element_type=jnp.float32)
    grad_low = jnp.einsum("pnr,pnd->prd", by_panel(down_low), rows_p, preferred_element_type=jnp.float32)
    grads_col = jnp.where(feature < width_loc, grad_up, grad_low)
    grads = lax.psum_scatter(
        grads_col.reshape(column * rank, width_loc + out_loc), "dz", scatter_dimension=0, tiled=True
    )
    grad_a = grads[:, :width_loc]
    grad_b = grads[:, width_loc:]
    grad_a = grad_a.astype(jnp.bfloat16).reshape(stored, rank, width_loc)
    grad_b = grad_b.astype(jnp.bfloat16).reshape(stored, rank, out_loc)

    base_bwd = jnp.einsum(
        "krc,dkc->rd",
        cot_parts,
        value_weight.reshape(width_loc, n_mp, out_loc),
        preferred_element_type=jnp.float32,
    )
    mine_back = jnp.take(back, position, axis=0, mode="clip").reshape(rows, width_loc + out_loc)
    values = (base_t.T + mine_back[:, width_loc:].astype(jnp.float32)).astype(jnp.bfloat16)
    token_gradient = (base_bwd + mine_back[:, :width_loc].astype(jnp.float32)).astype(jnp.bfloat16)
    return (values, token_gradient, grad_a, grad_b)


def split_dp(mesh):
    devices = np.asarray(mesh.devices)
    n_dp, n_mp = devices.shape
    try:
        n_x = len({tuple(d.coords)[0] for d in devices[:, 0]})
    except (AttributeError, TypeError):
        n_x = 1
    if n_x < 1 or n_dp % n_x:
        n_x = 1
    return Mesh(devices.reshape(n_dp // n_x, n_x, n_mp), ("dz", "dx", "mp"))


def solution(mesh):
    in_specs = (
        P(DP, "mp"),
        P("mp", None),
        P(DP, None, "mp"),
        P(DP, None, "mp"),
        P(DP, "mp"),
        P(DP),
        P(DP),
        P(),
    )
    out_specs = (P(DP, "mp"), P(DP, "mp"), P(DP, None, "mp"), P(DP, None, "mp"))
    return jax.shard_map(
        shards, mesh=split_dp(mesh), in_specs=in_specs, out_specs=out_specs, check_vma=False
    )
```

```python
import jax
import jax.numpy as jnp
import numpy as np
from jax import lax
from jax.sharding import Mesh
from jax.sharding import PartitionSpec as P

MOST = 2
DP = ("dz", "dx")
MP = ("my", "mc")


def earlier_same(group):
    count = group.shape[-1]
    ids = jnp.arange(count, dtype=jnp.int32)
    same = (group[..., :, None] == group[..., None, :]) & (ids[:, None] > ids[None, :])
    return jnp.sum(same.astype(jnp.int32), axis=-1)


def shards(
    tokens,
    value_weight,
    adapter_down_panels,
    adapter_up_panels,
    cotangent,
    block_list_entry,
    device_tenant_list,
    tenant_location_map,
):
    rows, width_loc = tokens.shape
    stored, rank, _ = adapter_down_panels.shape
    out_loc = adapter_up_panels.shape[2]
    blocks = block_list_entry.shape[0]
    blk = rows // blocks
    n_z = lax.axis_size("dz")
    n_x = lax.axis_size("dx")
    per_x = min(MOST * n_z, blocks)
    capacity = n_x * per_x
    my_x = lax.axis_index("dx")
    column = n_z * stored

    tenant = jnp.take(device_tenant_list, block_list_entry, mode="clip")
    location = jnp.take(tenant_location_map, tenant, mode="clip")
    owner_x = (location // stored) % n_x
    position = jnp.clip(owner_x * per_x + earlier_same(owner_x), 0, capacity - 1)

    slot_ids = jnp.arange(capacity, dtype=jnp.int32)
    block_ids = jnp.arange(blocks, dtype=jnp.int32)
    source = jnp.sum(
        jnp.where(position[None, :] == slot_ids[:, None], block_ids[None, :], 0), axis=1
    )

    base_part = lax.dot_general(
        value_weight, tokens, (((0,), (1,)), ((), ())), preferred_element_type=jnp.float32
    )
    location_tied, base_part = lax.optimization_barrier((location, base_part))
    base_t = lax.psum_scatter(base_part, MP, scatter_dimension=0, tiled=True)
    x_location = lax.all_gather(location_tied, "dx", axis=0, tiled=False)
    x_owner_x = (x_location // stored) % n_x
    x_rank = earlier_same(x_owner_x)
    in_column = (x_location // stored // n_x) * stored + x_location % stored
    mine = x_owner_x == my_x
    slot_panel = jnp.stack(
        [jnp.sum(jnp.where(mine & (x_rank == c), in_column + 1, 0), axis=1) for c in range(per_x)],
        axis=1,
    ).reshape(capacity) - 1
    panel_ids = jnp.arange(column, dtype=jnp.int32)
    slot_of = x_rank + (jnp.arange(n_x, dtype=jnp.int32) * per_x)[:, None]
    panel_slot = jnp.sum(
        jnp.where(
            mine[None, :, :] & (in_column[None, :, :] == panel_ids[:, None, None]),
            slot_of[None, :, :] + 1,
            0,
        ),
        axis=2,
    ) - 1
    panel_used = panel_slot >= 0
    panel_slot = jnp.clip(panel_slot, 0, capacity - 1)

    both_col = lax.all_gather(
        jnp.concatenate([adapter_down_panels, adapter_up_panels], axis=2), "dz", axis=0, tiled=True
    )
    down_col = both_col[:, :, :width_loc]
    up_col = both_col[:, :, width_loc:]

    n_mp = lax.axis_size("my") * lax.axis_size("mc")

    token_blocks = tokens.reshape(blocks, blk, width_loc)
    cot_blocks = cotangent.reshape(blocks, blk, out_loc)
    send = jnp.concatenate(
        [jnp.take(token_blocks, source, axis=0, mode="clip"), jnp.take(cot_blocks, source, axis=0, mode="clip")], axis=2
    )
    recv = lax.all_to_all(send, "dx", split_axis=0, concat_axis=0, tiled=True)
    tok_recv = recv[:, :, :width_loc]
    cot_recv = recv[:, :, width_loc:]

    panel_at = jnp.clip(slot_panel, 0, column - 1)
    down_sel = jnp.take(down_col, panel_at, axis=0, mode="clip")
    up_sel = jnp.take(up_col, panel_at, axis=0, mode="clip")
    down_part = jnp.einsum("snd,srd->snr", tok_recv, down_sel, preferred_element_type=jnp.float32)
    up_part = jnp.einsum("snc,src->snr", cot_recv, up_sel, preferred_element_type=jnp.float32)
    both = lax.psum(lax.psum(jnp.stack([down_part, up_part]), "mc"), "my").astype(jnp.bfloat16)
    cot_parts = lax.all_gather(cotangent, MP, axis=0, tiled=False)
    down_low = both[0]
    up_grad = both[1]

    adapter_out = jnp.einsum("snr,src->snc", down_low, up_sel, preferred_element_type=jnp.float32)
    adapter_bwd = jnp.einsum("snr,srd->snd", up_grad, down_sel, preferred_element_type=jnp.float32)
    back_send = jnp.concatenate(
        [adapter_bwd.astype(jnp.bfloat16), adapter_out.astype(jnp.bfloat16)], axis=2
    )
    back = lax.all_to_all(back_send, "dx", split_axis=0, concat_axis=0, tiled=True)

    def by_panel(small):
        small_p = jnp.take(small, panel_slot.reshape(-1), axis=0, mode="clip").reshape(column, n_x, blk, rank)
        small_p = jnp.where(panel_used[:, :, None, None], small_p, jnp.zeros_like(small_p))
        return small_p.reshape(column, n_x * blk, rank)

    rows_p = jnp.take(recv, panel_slot.reshape(-1), axis=0, mode="clip").reshape(
        column, n_x * blk, width_loc + out_loc
    )
    grad_up = jnp.einsum("pnr,pnd->prd", by_panel(up_grad), rows_p, preferred_element_type=jnp.float32)
    grad_low = jnp.einsum("pnr,pnd->prd", by_panel(down_low), rows_p, preferred_element_type=jnp.float32)
    feature = jnp.arange(width_loc + out_loc, dtype=jnp.int32)[None, None, :]
    grads_col = jnp.where(feature < width_loc, grad_up, grad_low)
    grads = lax.psum_scatter(
        grads_col.reshape(column * rank, width_loc + out_loc), "dz", scatter_dimension=0, tiled=True
    )
    grad_a = grads[:, :width_loc]
    grad_b = grads[:, width_loc:]
    grad_a = grad_a.astype(jnp.bfloat16).reshape(stored, rank, width_loc)
    grad_b = grad_b.astype(jnp.bfloat16).reshape(stored, rank, out_loc)

    base_bwd = jnp.einsum(
        "krc,dkc->rd",
        cot_parts,
        value_weight.reshape(width_loc, n_mp, out_loc),
        preferred_element_type=jnp.float32,
    )
    mine_back = jnp.take(back, position, axis=0, mode="clip").reshape(rows, width_loc + out_loc)
    values = (base_t.T + mine_back[:, width_loc:].astype(jnp.float32)).astype(jnp.bfloat16)
    token_gradient = (base_bwd + mine_back[:, :width_loc].astype(jnp.float32)).astype(jnp.bfloat16)
    return (values, token_gradient, grad_a, grad_b)


def split_dp(mesh):
    devices = np.asarray(mesh.devices)
    n_dp, n_mp = devices.shape
    try:
        n_x = len({tuple(d.coords)[0] for d in devices[:, 0]})
    except (AttributeError, TypeError):
        n_x = 1
    if n_x < 1 or n_dp % n_x:
        n_x = 1
    n_c = 2 if n_mp % 2 == 0 else 1
    return Mesh(devices.reshape(n_dp // n_x, n_x, n_mp // n_c, n_c), ("dz", "dx", "my", "mc"))


def solution(mesh):
    in_specs = (
        P(DP, MP),
        P(MP, None),
        P(DP, None, MP),
        P(DP, None, MP),
        P(DP, MP),
        P(DP),
        P(DP),
        P(),
    )
    out_specs = (P(DP, MP), P(DP, MP), P(DP, None, MP), P(DP, None, MP))
    return jax.shard_map(
        shards, mesh=split_dp(mesh), in_specs=in_specs, out_specs=out_specs, check_vma=False
    )
```

```python
import jax
import jax.numpy as jnp
import numpy as np
from jax import lax
from jax.sharding import Mesh
from jax.sharding import PartitionSpec as P

MOST = 2
DP = ("dz", "dx")


def earlier_same(group):
    count = group.shape[-1]
    ids = jnp.arange(count, dtype=jnp.int32)
    same = (group[..., :, None] == group[..., None, :]) & (ids[:, None] > ids[None, :])
    return jnp.sum(same.astype(jnp.int32), axis=-1)


def shards(
    tokens,
    value_weight,
    adapter_down_panels,
    adapter_up_panels,
    cotangent,
    block_list_entry,
    device_tenant_list,
    tenant_location_map,
):
    rows, width_loc = tokens.shape
    stored, rank, _ = adapter_down_panels.shape
    out_loc = adapter_up_panels.shape[2]
    blocks = block_list_entry.shape[0]
    blk = rows // blocks
    n_z = lax.axis_size("dz")
    n_x = lax.axis_size("dx")
    per_x = min(MOST * n_z, blocks)
    capacity = n_x * per_x
    my_x = lax.axis_index("dx")
    column = n_z * stored

    tenant = jnp.take(device_tenant_list, block_list_entry, mode="clip")
    location = jnp.take(tenant_location_map, tenant, mode="clip")
    owner_x = (location // stored) % n_x
    position = jnp.clip(owner_x * per_x + earlier_same(owner_x), 0, capacity - 1)

    slot_ids = jnp.arange(capacity, dtype=jnp.int32)
    block_ids = jnp.arange(blocks, dtype=jnp.int32)
    source = jnp.sum(
        jnp.where(position[None, :] == slot_ids[:, None], block_ids[None, :], 0), axis=1
    )

    base_part = lax.dot_general(
        value_weight, tokens, (((0,), (1,)), ((), ())), preferred_element_type=jnp.float32
    )
    location_tied, base_part = lax.optimization_barrier((location, base_part))
    base_t = lax.psum_scatter(base_part, "mp", scatter_dimension=0, tiled=True)
    x_location = lax.all_gather(location_tied, "dx", axis=0, tiled=False)
    x_owner_x = (x_location // stored) % n_x
    x_rank = earlier_same(x_owner_x)
    in_column = (x_location // stored // n_x) * stored + x_location % stored
    mine = x_owner_x == my_x
    slot_panel = jnp.stack(
        [jnp.sum(jnp.where(mine & (x_rank == c), in_column + 1, 0), axis=1) for c in range(per_x)],
        axis=1,
    ).reshape(capacity) - 1
    panel_ids = jnp.arange(column, dtype=jnp.int32)
    slot_of = x_rank + (jnp.arange(n_x, dtype=jnp.int32) * per_x)[:, None]
    panel_slot = jnp.sum(
        jnp.where(
            mine[None, :, :] & (in_column[None, :, :] == panel_ids[:, None, None]),
            slot_of[None, :, :] + 1,
            0,
        ),
        axis=2,
    ) - 1
    panel_used = panel_slot >= 0
    panel_slot = jnp.clip(panel_slot, 0, capacity - 1)

    both_col = lax.all_gather(
        jnp.concatenate([adapter_down_panels, adapter_up_panels], axis=2), "dz", axis=0, tiled=True
    )
    down_col = both_col[:, :, :width_loc]
    up_col = both_col[:, :, width_loc:]

    n_mp = lax.axis_size("mp")

    token_blocks = tokens.reshape(blocks, blk, width_loc)
    cot_blocks = cotangent.reshape(blocks, blk, out_loc)
    send = jnp.concatenate(
        [jnp.take(token_blocks, source, axis=0, mode="clip"), jnp.take(cot_blocks, source, axis=0, mode="clip")], axis=2
    )
    recv = lax.all_to_all(send, "dx", split_axis=0, concat_axis=0, tiled=True)
    tok_recv = recv[:, :, :width_loc]
    cot_recv = recv[:, :, width_loc:]

    panel_at = jnp.clip(slot_panel, 0, column - 1)
    down_sel = jnp.take(down_col, panel_at, axis=0, mode="clip")
    up_sel = jnp.take(up_col, panel_at, axis=0, mode="clip")
    down_part = jnp.einsum("snd,srd->snr", tok_recv, down_sel, preferred_element_type=jnp.float32)
    up_part = jnp.einsum("snc,src->snr", cot_recv, up_sel, preferred_element_type=jnp.float32)
    both = lax.psum(jnp.stack([down_part, up_part]), "mp").astype(jnp.bfloat16)
    cot_parts = lax.all_gather(cotangent, "mp", axis=0, tiled=False)
    down_low = both[0]
    up_grad = both[1]

    adapter_out = jnp.einsum("snr,src->snc", down_low, up_sel, preferred_element_type=jnp.float32)
    adapter_bwd = jnp.einsum("snr,srd->snd", up_grad, down_sel, preferred_element_type=jnp.float32)
    back_send = jnp.concatenate(
        [adapter_bwd.astype(jnp.bfloat16), adapter_out.astype(jnp.bfloat16)], axis=2
    )
    back = lax.all_to_all(back_send, "dx", split_axis=0, concat_axis=0, tiled=True)

    def by_panel(small):
        small_p = jnp.take(small, panel_slot.reshape(-1), axis=0, mode="clip").reshape(column, n_x, blk, rank)
        small_p = jnp.where(panel_used[:, :, None, None], small_p, jnp.zeros_like(small_p))
        return small_p.reshape(column, n_x * blk, rank)

    rows_p = jnp.take(recv, panel_slot.reshape(-1), axis=0, mode="clip").reshape(
        column, n_x * blk, width_loc + out_loc
    )
    grad_up = jnp.einsum("pnr,pnd->prd", by_panel(up_grad), rows_p, preferred_element_type=jnp.float32)
    grad_low = jnp.einsum("pnr,pnd->prd", by_panel(down_low), rows_p, preferred_element_type=jnp.float32)
    feature = jnp.arange(width_loc + out_loc, dtype=jnp.int32)[None, None, :]
    grads_col = jnp.where(feature < width_loc, grad_up, grad_low)
    grads = lax.psum_scatter(
        grads_col.astype(jnp.bfloat16).reshape(column * rank, width_loc + out_loc),
        "dz",
        scatter_dimension=0,
        tiled=True,
    )
    grad_a = grads[:, :width_loc]
    grad_b = grads[:, width_loc:]
    grad_a = grad_a.astype(jnp.bfloat16).reshape(stored, rank, width_loc)
    grad_b = grad_b.astype(jnp.bfloat16).reshape(stored, rank, out_loc)

    base_bwd = jnp.einsum(
        "krc,dkc->rd",
        cot_parts,
        value_weight.reshape(width_loc, n_mp, out_loc),
        preferred_element_type=jnp.float32,
    )
    base_bwd = lax.optimization_barrier(base_bwd)
    mine_back = jnp.take(back, position, axis=0, mode="clip").reshape(rows, width_loc + out_loc)
    values = (base_t.T + mine_back[:, width_loc:].astype(jnp.float32)).astype(jnp.bfloat16)
    token_gradient = (base_bwd + mine_back[:, :width_loc].astype(jnp.float32)).astype(jnp.bfloat16)
    return (values, token_gradient, grad_a, grad_b)


def split_dp(mesh):
    devices = np.asarray(mesh.devices)
    n_dp, n_mp = devices.shape
    try:
        n_x = len({tuple(d.coords)[0] for d in devices[:, 0]})
    except (AttributeError, TypeError):
        n_x = 1
    if n_x < 1 or n_dp % n_x:
        n_x = 1
    return Mesh(devices.reshape(n_dp // n_x, n_x, n_mp), ("dz", "dx", "mp"))


def solution(mesh):
    in_specs = (
        P(DP, "mp"),
        P("mp", None),
        P(DP, None, "mp"),
        P(DP, None, "mp"),
        P(DP, "mp"),
        P(DP),
        P(DP),
        P(),
    )
    out_specs = (P(DP, "mp"), P(DP, "mp"), P(DP, None, "mp"), P(DP, None, "mp"))
    return jax.shard_map(
        shards, mesh=split_dp(mesh), in_specs=in_specs, out_specs=out_specs, check_vma=False
    )
```

```python
import jax
import jax.numpy as jnp
import numpy as np
from jax import lax
from jax.sharding import Mesh
from jax.sharding import PartitionSpec as P

MOST = 2
DP = ("dz", "dx")


def earlier_same(group):
    count = group.shape[-1]
    ids = jnp.arange(count, dtype=jnp.int32)
    same = (group[..., :, None] == group[..., None, :]) & (ids[:, None] > ids[None, :])
    return jnp.sum(same.astype(jnp.int32), axis=-1)


def shards(
    tokens,
    value_weight,
    adapter_down_panels,
    adapter_up_panels,
    cotangent,
    block_list_entry,
    device_tenant_list,
    tenant_location_map,
):
    rows, width_loc = tokens.shape
    stored, rank, _ = adapter_down_panels.shape
    out_loc = adapter_up_panels.shape[2]
    blocks = block_list_entry.shape[0]
    blk = rows // blocks
    n_z = lax.axis_size("dz")
    n_x = lax.axis_size("dx")
    per_x = min(MOST * n_z, blocks)
    capacity = n_x * per_x
    my_x = lax.axis_index("dx")
    column = n_z * stored

    tenant = jnp.take(device_tenant_list, block_list_entry, mode="clip")
    location = jnp.take(tenant_location_map, tenant, mode="clip")
    owner_x = (location // stored) % n_x
    position = jnp.clip(owner_x * per_x + earlier_same(owner_x), 0, capacity - 1)

    slot_ids = jnp.arange(capacity, dtype=jnp.int32)
    block_ids = jnp.arange(blocks, dtype=jnp.int32)
    source = jnp.sum(
        jnp.where(position[None, :] == slot_ids[:, None], block_ids[None, :], 0), axis=1
    )

    base_part = lax.dot_general(
        value_weight, tokens, (((0,), (1,)), ((), ())), preferred_element_type=jnp.float32
    )
    location_tied, base_part = lax.optimization_barrier((location, base_part))
    base_t = lax.psum_scatter(base_part, "mp", scatter_dimension=0, tiled=True)
    x_location = lax.all_gather(location_tied, "dx", axis=0, tiled=False)
    x_owner_x = (x_location // stored) % n_x
    x_rank = earlier_same(x_owner_x)
    in_column = (x_location // stored // n_x) * stored + x_location % stored
    mine = x_owner_x == my_x
    slot_panel = jnp.stack(
        [jnp.sum(jnp.where(mine & (x_rank == c), in_column + 1, 0), axis=1) for c in range(per_x)],
        axis=1,
    ).reshape(capacity) - 1
    panel_ids = jnp.arange(column, dtype=jnp.int32)
    slot_of = x_rank + (jnp.arange(n_x, dtype=jnp.int32) * per_x)[:, None]
    panel_slot = jnp.sum(
        jnp.where(
            mine[None, :, :] & (in_column[None, :, :] == panel_ids[:, None, None]),
            slot_of[None, :, :] + 1,
            0,
        ),
        axis=2,
    ) - 1
    panel_used = panel_slot >= 0
    panel_slot = jnp.clip(panel_slot, 0, capacity - 1)

    both_col = lax.all_gather(
        jnp.concatenate([adapter_down_panels, adapter_up_panels], axis=2), "dz", axis=0, tiled=True
    )
    down_col = both_col[:, :, :width_loc]
    up_col = both_col[:, :, width_loc:]

    n_mp = lax.axis_size("mp")

    token_blocks = tokens.reshape(blocks, blk, width_loc)
    cot_blocks = cotangent.reshape(blocks, blk, out_loc)
    send = jnp.concatenate(
        [jnp.take(token_blocks, source, axis=0, mode="clip"), jnp.take(cot_blocks, source, axis=0, mode="clip")], axis=2
    )
    recv = lax.all_to_all(send, "dx", split_axis=0, concat_axis=0, tiled=True)
    tok_recv = recv[:, :, :width_loc]
    cot_recv = recv[:, :, width_loc:]

    panel_at = jnp.clip(slot_panel, 0, column - 1)
    down_sel = jnp.take(down_col, panel_at, axis=0, mode="clip")
    up_sel = jnp.take(up_col, panel_at, axis=0, mode="clip")
    down_part = jnp.einsum("snd,srd->snr", tok_recv, down_sel, preferred_element_type=jnp.float32)
    up_part = jnp.einsum("snc,src->snr", cot_recv, up_sel, preferred_element_type=jnp.float32)
    both = lax.psum(jnp.stack([down_part, up_part]), "mp").astype(jnp.bfloat16)
    cot_parts = lax.all_gather(cotangent, "mp", axis=0, tiled=False)
    down_low = both[0]
    up_grad = both[1]

    adapter_out = jnp.einsum("snr,src->snc", down_low, up_sel, preferred_element_type=jnp.float32)
    adapter_bwd = jnp.einsum("snr,srd->snd", up_grad, down_sel, preferred_element_type=jnp.float32)
    back_send = jnp.concatenate(
        [adapter_bwd.astype(jnp.bfloat16), adapter_out.astype(jnp.bfloat16)], axis=2
    )
    back = lax.all_to_all(back_send, "dx", split_axis=0, concat_axis=0, tiled=True)

    def by_panel(small):
        small_p = jnp.take(small, panel_slot.reshape(-1), axis=0, mode="clip").reshape(column, n_x, blk, rank)
        small_p = jnp.where(panel_used[:, :, None, None], small_p, jnp.zeros_like(small_p))
        return small_p.reshape(column, n_x * blk, rank)

    rows_p = jnp.take(recv, panel_slot.reshape(-1), axis=0, mode="clip").reshape(
        column, n_x * blk, width_loc + out_loc
    )
    grad_up = jnp.einsum("pnr,pnd->prd", by_panel(up_grad), rows_p, preferred_element_type=jnp.float32)
    grad_low = jnp.einsum("pnr,pnd->prd", by_panel(down_low), rows_p, preferred_element_type=jnp.float32)
    feature = jnp.arange(width_loc + out_loc, dtype=jnp.int32)[None, None, :]
    grads_col = jnp.where(feature < width_loc, grad_up, grad_low)
    grads = lax.psum_scatter(
        grads_col.reshape(column * rank, width_loc + out_loc), "dz", scatter_dimension=0, tiled=True
    )
    grad_a = grads[:, :width_loc]
    grad_b = grads[:, width_loc:]
    grad_a = grad_a.astype(jnp.bfloat16).reshape(stored, rank, width_loc)
    grad_b = grad_b.astype(jnp.bfloat16).reshape(stored, rank, out_loc)

    base_bwd = jnp.einsum(
        "krc,dkc->rd",
        cot_parts,
        value_weight.reshape(width_loc, n_mp, out_loc),
        preferred_element_type=jnp.float32,
    )
    base_bwd = lax.optimization_barrier(base_bwd)
    mine_back = jnp.take(back, position, axis=0, mode="clip").reshape(rows, width_loc + out_loc)
    values = (base_t.T + mine_back[:, width_loc:].astype(jnp.float32)).astype(jnp.bfloat16)
    token_gradient = (base_bwd + mine_back[:, :width_loc].astype(jnp.float32)).astype(jnp.bfloat16)
    return (values, token_gradient, grad_a, grad_b)


def split_dp(mesh):
    devices = np.asarray(mesh.devices)
    n_dp, n_mp = devices.shape
    try:
        n_x = len({tuple(d.coords)[0] for d in devices[:, 0]})
    except (AttributeError, TypeError):
        n_x = 1
    if n_x < 1 or n_dp % n_x:
        n_x = 1
    return Mesh(devices.reshape(n_dp // n_x, n_x, n_mp), ("dz", "dx", "mp"))


def solution(mesh):
    in_specs = (
        P(DP, "mp"),
        P("mp", None),
        P(DP, None, "mp"),
        P(DP, None, "mp"),
        P(DP, "mp"),
        P(DP),
        P(DP),
        P(),
    )
    out_specs = (P(DP, "mp"), P(DP, "mp"), P(DP, None, "mp"), P(DP, None, "mp"))
    return jax.shard_map(
        shards, mesh=split_dp(mesh), in_specs=in_specs, out_specs=out_specs, check_vma=False
    )
```
